128 devices in a mesh: elem: 8 (over z, core), vox: 16 (over y, x).
Axes of the slice: x: 4, y: 4, z: 4, core: 2. Of those that a mesh axis runs over, the one named last changes fastest.
Arguments:
- echoes: bfloat16 [1024, 2, 64, 2048], P(('elem', 'vox')), may hold values from -12 to 12, as said below
- filter_taps: bfloat16 [2, 16], replicated, may hold values from -1.5 to 1.5
- visible: int32 [128, 128, 2], replicated, may hold values from -1 to 7, as said below
- window_start: int32 [2, 128, 128, 2], P(None, None, ('elem', 'vox')), may hold values from 0 to 384
- delays: int32 [2, 128, 128, 2, 1536], P(None, ('elem', 'vox')), may hold values from 0 to 507
- tile_gain: float32 [128], P(('elem', 'vox')), may hold values from 0.5 to 12, as said below
Outputs:
- doppler_power: float32 [128, 1536], P(('elem', 'vox'))
The draws below stay inside these ranges and needn't reach their ends.
Inputs may be any that keep to these rules, and one draw needn't show every extreme that they name: `echoes`: echoes are blood signal plus a stronger tissue part that has few patterns over frames. `visible`: -1 marks an empty slot; the live entries of one tile and block are distinct; a tile has at most 192 live slots, some tile exactly 192, and in that tile one block fills all 2 of its slots. `tile_gain`: positive gains.
All inputs are finite; a program needn't handle non-finite values.
Results may differ from the reference program's by a relative error of at most 0.0004.
Values may be sent and summed in bfloat16 or wider, within the bound.
No kernel may reach another device: no remote copies, remote signals or barrier semaphores. Data moves between devices by JAX's collectives and lax.ppermute only.
A program may use at most 128 MiB of HBM per device.

```python
import jax
import jax.numpy as jnp
from jax import lax

E_DEV = 8
PW = 2
FRAMES = 64
TAPS = 16
W = 128
CAP = 2
NS = 512
V = 1536
ELEMS = 1024
SAMPLES = 2048
BLOCKS = 128
TILES = 128
SLOTS = 256
MOST = 192


def draw_echoes(key, part):
    subkeys = jax.random.split(key, 3)
    full_shape = (ELEMS, PW, FRAMES, SAMPLES)
    blood_echo = jax.random.normal(subkeys[0], full_shape, jnp.float32)
    amplitude = jax.random.normal(subkeys[1], (3, ELEMS, PW, 1, SAMPLES), jnp.float32)
    temporal = jax.random.normal(subkeys[2], (3, 1, 1, FRAMES, 1), jnp.float32)
    tissue = amplitude[0] * temporal[0] + amplitude[1] * temporal[1] + amplitude[2] * temporal[2]
    return jnp.clip(blood_echo + tissue, -12.0, 12.0).astype(jnp.bfloat16)


def draw_tile_gain(key, part):
    position = jnp.arange(TILES, dtype=jnp.float32) / max(TILES - 1, 1)
    depth_ramp = jnp.exp(position * jnp.log(3.0))
    jitter = jax.random.uniform(key, (TILES,), jnp.float32, 0.8, 1.25)
    return (depth_ramp * jitter).astype(jnp.float32)


def draw_visible(key, part):
    subkeys = jax.random.split(key, 5)
    tile_ids = jnp.arange(TILES, dtype=jnp.int32)
    levels = jax.random.randint(subkeys[0], (TILES,), MOST * 2 // 3, MOST + 1)
    chosen = jax.random.randint(subkeys[1], (), 0, TILES)
    counts = jnp.where(tile_ids == chosen, MOST, levels)
    tile_keys = jax.random.split(subkeys[2], TILES)
    shuffled = jax.vmap(lambda single: jax.random.permutation(single, SLOTS))(tile_keys).astype(jnp.int32)
    full_block = jax.random.randint(subkeys[3], (), 0, BLOCKS)
    in_block = jnp.arange(SLOTS, dtype=jnp.int32) // CAP == full_block
    scores = jnp.where((tile_ids[:, None] == chosen) & in_block[None, :], shuffled - SLOTS, shuffled)
    slot_order = jnp.argsort(jnp.argsort(scores, axis=1, stable=True), axis=1, stable=True)
    live_slots = (slot_order < counts[:, None]).reshape(TILES, BLOCKS, CAP)
    starts = jax.random.randint(subkeys[4], (TILES, BLOCKS, 1), 0, E_DEV)
    element = (starts + jnp.arange(CAP, dtype=jnp.int32)[None, None, :]) % E_DEV
    return jnp.where(live_slots, element, -1).astype(jnp.int32)


def place_ends(drawn, rng, least, largest):
    spot = [jax.random.randint(jax.random.fold_in(rng, axis), (), 0, length) for axis, length in enumerate(drawn.shape)]
    longest = drawn.shape.index(max(drawn.shape))
    next_to = spot[:longest] + [(spot[longest] + 1) % drawn.shape[longest]] + spot[longest + 1:]
    return drawn.at[tuple(spot)].set(least).at[tuple(next_to)].set(largest)


def centred(rng, dims, spread, limit, kind=jnp.bfloat16):
    return jnp.clip(spread * jax.random.normal(rng, dims, jnp.float32), -limit, limit).astype(kind)


def setup_inputs(seed: int = 0) -> dict:
    streams_of = jax.random.split(jax.random.key(seed), 7)
    return {
        "echoes": draw_echoes(jax.random.fold_in(streams_of[6], 71), 0),
        "filter_taps": centred(streams_of[1], (2, TAPS), 0.25, 1.5),
        "visible": draw_visible(jax.random.fold_in(streams_of[6], 71), 0),
        "window_start": place_ends(jax.random.randint(streams_of[3], (PW, TILES, BLOCKS, CAP), 0, NS - W + 1), jax.random.fold_in(streams_of[3], 1), 0, NS - W).astype(jnp.int32),
        "delays": place_ends(jax.random.randint(streams_of[4], (PW, TILES, BLOCKS, CAP, V), 0, 4 * (W - 1)), jax.random.fold_in(streams_of[4], 1), 0, (4 * (W - 1)) - 1).astype(jnp.int32),
        "tile_gain": draw_tile_gain(jax.random.fold_in(streams_of[6], 71), 0),
    }


damping = 0.5

def demodulate(element_block, filter_taps):
    members, planes, frames, samples = element_block.shape
    decimated = samples // 4
    quarter = filter_taps.shape[1] // 4
    grouped = element_block.astype(jnp.float32).reshape(members, planes, frames, decimated, 4)
    grouped = jnp.pad(grouped, ((0, 0), (0, 0), (0, 0), (0, quarter - 1), (0, 0)))
    tap_table = filter_taps.astype(jnp.float32).reshape(2, quarter, 4)
    summed = jnp.zeros((members, planes, decimated, 2, frames), jnp.float32)
    for tap_group in range(quarter):
        summed = summed + jnp.einsum('epfnr,cr->epncf', grouped[:, :, :, tap_group:tap_group + decimated, :], tap_table[:, tap_group, :], precision=lax.Precision.HIGHEST)
    return summed.reshape(members, planes, decimated, 2 * frames).astype(jnp.bfloat16)

def reference(echoes, filter_taps, visible, window_start, delays, tile_gain):
    channels = 2 * FRAMES
    blocked = echoes.reshape(BLOCKS, E_DEV, PW, FRAMES, SAMPLES)

    def demod_block(element_block):
        return demodulate(element_block, filter_taps)
    baseband = lax.map(demod_block, blocked).reshape(ELEMS, PW, NS, channels)
    start_table = jnp.transpose(window_start, (1, 0, 2, 3))
    lag_all = jnp.transpose(delays, (1, 0, 2, 3, 4))

    def one_tile(inputs):
        seen_slots, starts, lag_table, tile_scale = inputs
        element = (jnp.arange(BLOCKS, dtype=jnp.int32)[:, None] * E_DEV + jnp.maximum(seen_slots, 0)).reshape(SLOTS).astype(jnp.int32)
        live_slots = (seen_slots >= 0).reshape(SLOTS)
        starts = starts.reshape(PW, SLOTS).astype(jnp.int32)
        lag_table = lag_table.reshape(PW, SLOTS, V).astype(jnp.int32)

        def add_slot(summed, slot_index):
            elem_id = element[slot_index]
            for plane_index in range(PW):
                window = lax.dynamic_slice(baseband, (elem_id, jnp.int32(plane_index), starts[plane_index, slot_index], jnp.int32(0)), (1, 1, W, channels))[0, 0].astype(jnp.float32)
                lag_row = lag_table[plane_index, slot_index]
                floor_row = lag_row // 4
                fraction = (lag_row - 4 * floor_row).astype(jnp.float32) * 0.25
                contribution = (1.0 - fraction)[:, None] * window[floor_row] + fraction[:, None] * window[floor_row + 1]
                summed = summed + jnp.where(live_slots[slot_index], contribution, jnp.zeros_like(contribution))
            return (summed, None)
        summed, unused = lax.scan(add_slot, jnp.zeros((V, channels), jnp.float32), jnp.arange(SLOTS, dtype=jnp.int32))
        return summed * tile_scale
    beams = lax.map(one_tile, (visible, start_table, lag_all, tile_gain))
    flat_beams = beams.reshape(TILES * V, channels)
    frame_gram = jnp.dot(flat_beams.T, flat_beams, precision=lax.Precision.HIGHEST)
    energy = jnp.trace(frame_gram)
    correlation = frame_gram * (channels / energy)
    identity = jnp.eye(channels, dtype=jnp.float32)
    factor = jnp.linalg.cholesky(correlation + damping * identity)
    half_solve = lax.linalg.triangular_solve(factor, damping * identity, left_side=True, lower=True)
    filter_matrix = lax.linalg.triangular_solve(factor, half_solve, left_side=True, lower=True, transpose_a=True)
    norm_scale = jnp.sqrt(energy / (channels * TILES * V))
    filtered = jnp.dot(flat_beams, filter_matrix, precision=lax.Precision.HIGHEST) / norm_scale
    log_power = jnp.log(lax.optimization_barrier(jnp.mean(filtered * filtered, axis=-1)) + 1e-06)
    return log_power.reshape(TILES, V)
```

```python
import jax
import jax.numpy as jnp
from jax import lax
from jax.experimental import pallas as pl
from jax.experimental.pallas import tpu as pltpu
from jax.sharding import PartitionSpec as P

W = 128
damping = 0.5
AXES = ("elem", "vox")
BF, F32 = jnp.bfloat16, jnp.float32

FIRST = ((0, 0), (0, 1), (1, 0))
SECOND = ((1, 1),)
TILES_PER_STEP = 8


def window_kernel(elem_ref, start_ref, band_ref, echo_ref, first_ref, second_ref, base_ref):
    step = pl.program_id(0)
    members = base_ref.shape[0]

    @pl.when(step < members)
    def _():
        rows = []
        for plane in range(2):
            x = echo_ref[0, plane]
            x = jnp.concatenate([x, jnp.zeros((x.shape[0], 128), x.dtype)], axis=1)
            for j in range(4):
                rows.append(x[:, 512 * j : 512 * j + 640])
        out = jnp.dot(jnp.concatenate(rows, axis=0), band_ref[...], preferred_element_type=F32)
        out = out.astype(BF).astype(F32)
        for plane in range(2):
            for j in range(4):
                r = 64 * (4 * plane + j)
                base_ref[step, plane, j, 0:64, :] = out[r : r + 64, 0:128]
                base_ref[step, plane, j, 64:128, :] = out[r : r + 64, 128:256]

    @pl.when(step >= members)
    def _():
        lane = lax.broadcasted_iota(jnp.int32, (128, 128), 1)

        def one_tile(i, carry):
            tile = (step - members) * TILES_PER_STEP + i
            for ref, units in ((first_ref, FIRST), (second_ref, SECOND)):
                for k, (slot, plane) in enumerate(units):
                    seen = elem_ref[tile * 2 + slot]
                    member = jnp.maximum(seen, 0)
                    start = start_ref[(plane * 128 + tile) * 2 + slot]
                    block = start // 128
                    shift = start - 128 * block
                    here = base_ref[member, plane, block]
                    after = base_ref[member, plane, jnp.minimum(block + 1, 3)]
                    both = jnp.where(lane >= shift, here, after)
                    out = pltpu.roll(both, (128 - shift) & 127, 1)
                    out = jnp.where(seen >= 0, out, 0.0)
                    ref[i, k] = out.astype(BF)
            return carry

        lax.fori_loop(0, TILES_PER_STEP, one_tile, 0)


def make_windows(echoes, band, seen, starts):
    members, planes, frames, samples = echoes.shape
    tiles = seen.shape[0] // 2
    steps = members + tiles // TILES_PER_STEP
    last = members - 1

    def out_map(i, *_):
        return (jnp.maximum(i - members, 0), 0, 0, 0)

    return pl.pallas_call(
        window_kernel,
        grid_spec=pltpu.PrefetchScalarGridSpec(
            num_scalar_prefetch=2,
            grid=(steps,),
            in_specs=[
                pl.BlockSpec(band.shape, lambda i, *_: (0, 0)),
                pl.BlockSpec((1, planes, frames, samples), lambda i, *_: (jnp.minimum(i, last), 0, 0, 0)),
            ],
            out_specs=[
                pl.BlockSpec((TILES_PER_STEP, len(FIRST), 128, 128), out_map),
                pl.BlockSpec((TILES_PER_STEP, len(SECOND), 128, 128), out_map),
            ],
            scratch_shapes=[pltpu.VMEM((members, planes, 4, 128, 128), F32)],
        ),
        out_shape=[
            jax.ShapeDtypeStruct((tiles, len(FIRST), 128, 128), BF),
            jax.ShapeDtypeStruct((tiles, len(SECOND), 128, 128), BF),
        ],
        compiler_params=pltpu.CompilerParams(vmem_limit_bytes=48 * 2**20),
        cost_estimate=pl.CostEstimate(flops=2 * 10**9, bytes_accessed=24 * 2**20, transcendentals=0),
        name="windows",
    )(seen, starts, band, echoes)


def build_weights(out_ref, row, lag):
    lag = jnp.broadcast_to(lag.astype(F32) * 0.25 - 64.0, (16, lag.shape[1])).astype(BF)
    iota = lax.broadcasted_iota(jnp.int32, (16, 128), 0).astype(F32)
    rows = [(iota + (16.0 * w - 64.0)).astype(BF) for w in range(8)]
    one, zero = jnp.ones((), BF), jnp.zeros((), BF)
    for c in range(lag.shape[1] // 128):
        d = lag[:, 128 * c : 128 * c + 128]
        for w in range(8):
            out_ref[row + 16 * w : row + 16 * w + 16, 128 * c : 128 * c + 128] = jnp.maximum(
                one - jnp.abs(d - rows[w]), zero
            )


def accumulate(units, group, chunk, windows_ref, lag_ref, acc_ref, weight_ref):
    todo = [(b, k) for b in range(group) for k in range(len(units))]
    for n, at in enumerate(range(0, len(todo), chunk)):
        part = todo[at : at + chunk]
        half = weight_ref.at[n % 2]
        for m, (b, k) in enumerate(part):
            slot, plane = units[k]
            build_weights(half, 128 * m, lag_ref[plane, b, slot : slot + 1, :])
        lhs = jnp.concatenate([windows_ref[b, k] for b, k in part], axis=1)
        acc_ref[...] += jnp.dot(lhs, half[...], preferred_element_type=F32)


def first_beam_kernel(units, group, chunk, lag_ref, windows_ref, out_ref, weight_ref):
    @pl.when(pl.program_id(0) == 0)
    def _():
        out_ref[...] = jnp.zeros_like(out_ref)

    accumulate(units, group, chunk, windows_ref, lag_ref, out_ref, weight_ref)


def second_beam_kernel(units, group, chunk, gain_ref, lag_ref, windows_ref, before_ref, out_ref, gram_ref, weight_ref):
    @pl.when(pl.program_id(0) == 0)
    def _():
        out_ref[...] = before_ref[...]

    accumulate(units, group, chunk, windows_ref, lag_ref, out_ref, weight_ref)

    @pl.when(pl.program_id(0) == pl.num_programs(0) - 1)
    def _():
        beam = out_ref[...] * gain_ref[0]
        out_ref[...] = beam
        gram_ref[...] = lax.dot_general(
            beam, beam, (((1,), (1,)), ((), ())), precision=lax.Precision.HIGHEST, preferred_element_type=F32
        )


def beam_call(units, group, chunk, lags, windows, gain=None, before=None):
    planes, blocks, slots, voxels = lags.shape
    body = second_beam_kernel if before is not None else first_beam_kernel
    in_specs = [
        pl.BlockSpec((planes, group, slots, voxels), lambda i: (0, i, 0, 0)),
        pl.BlockSpec((group, len(units), 128, 128), lambda i: (i, 0, 0, 0)),
    ]
    args = [lags, windows]
    whole = pl.BlockSpec((128, voxels), lambda i: (0, 0))
    out_shape = [jax.ShapeDtypeStruct((128, voxels), F32)]
    out_specs = [whole]
    if before is not None:
        in_specs = [pl.BlockSpec(memory_space=pltpu.SMEM)] + in_specs + [whole]
        args = [gain] + args + [before]
        out_shape.append(jax.ShapeDtypeStruct((128, 128), F32))
        out_specs.append(pl.BlockSpec((128, 128), lambda i: (0, 0)))

    def kernel(*refs):
        body(units, group, chunk, *refs)

    return pl.pallas_call(
        kernel,
        grid=(blocks // group,),
        in_specs=in_specs,
        out_specs=out_specs,
        out_shape=out_shape,
        scratch_shapes=[pltpu.VMEM((2, 128 * chunk, voxels), BF)],
        compiler_params=pltpu.CompilerParams(vmem_limit_bytes=48 * 2**20),
        cost_estimate=pl.CostEstimate(
            flops=2 * 128 * voxels * 128 * blocks * len(units),
            bytes_accessed=blocks * len(units) * (128 * 256 + 8 * voxels),
            transcendentals=0,
        ),
        name="beam",
    )(*args)


def exchange_sum(x):
    for axis, digits in (("elem", (1,)), ("elem", (2, 4, 6)), ("vox", (1, 2, 3)), ("vox", (4, 8, 12))):
        size = lax.axis_size(axis)
        parts = [lax.ppermute(x, axis, [(i, i ^ k) for i in range(size)]) for k in digits]
        for part in parts:
            x = x + part
    return x


def shards(echoes, filter_taps, visible, window_start, delays, tile_gain):
    members, planes, frames, samples = echoes.shape
    channels = 2 * frames
    device_count = lax.axis_size("elem") * lax.axis_size("vox")
    voxels = delays.shape[-1]
    my_index = lax.axis_index(AXES)

    offset = (
        lax.broadcasted_iota(jnp.int32, (640, 2, 128), 0) - 4 * lax.broadcasted_iota(jnp.int32, (640, 2, 128), 2)
    )
    band = jnp.zeros((640, 2, 128), BF)
    for k in range(filter_taps.shape[1]):
        band = jnp.where(offset == k, filter_taps[None, :, k : k + 1], band)
    band = band.reshape(640, 256)

    seen = lax.dynamic_index_in_dim(visible, my_index, 1, keepdims=False).reshape(-1)
    starts = window_start[:, :, 0, :].reshape(-1)
    first, second = make_windows(echoes, band, seen, starts)

    first = lax.all_to_all(first, AXES, split_axis=0, concat_axis=0, tiled=True)
    second = lax.all_to_all(second, AXES, split_axis=0, concat_axis=0, tiled=True)
    lags = delays[:, 0]
    (partial,) = beam_call(FIRST, 4, 4, lags, first)
    beam, local_gram = beam_call(SECOND, 8, 4, lags, second, tile_gain, partial)

    frame_gram = exchange_sum(local_gram)
    energy = jnp.trace(frame_gram)
    correlation = frame_gram * (channels / energy)
    identity = jnp.eye(channels, dtype=F32)
    factor = jnp.linalg.cholesky(correlation + damping * identity)
    half_solve = lax.linalg.triangular_solve(factor, damping * identity, left_side=True, lower=True)
    filter_matrix = lax.linalg.triangular_solve(
        factor, half_solve, left_side=True, lower=True, transpose_a=True
    )
    norm_scale = jnp.sqrt(energy / (channels * device_count * voxels))
    filtered = jnp.dot(filter_matrix, beam, precision=lax.Precision.HIGHEST) / norm_scale
    log_power = jnp.log(jnp.mean(filtered * filtered, axis=0) + 1e-06)
    return log_power.reshape(1, voxels)


def solution(mesh):
    placed = (
        P(AXES, None, None, None),
        P(),
        P(),
        P(None, None, AXES, None),
        P(None, AXES, None, None, None),
        P(AXES),
    )
    return jax.shard_map(
        shards, mesh=mesh, in_specs=placed, out_specs=P(AXES, None), check_vma=False
    )
```

```python
import jax
import jax.numpy as jnp
from jax import lax
from jax.experimental import pallas as pl
from jax.experimental.pallas import tpu as pltpu
from jax.sharding import PartitionSpec as P

W = 128
damping = 0.5
AXES = ("elem", "vox")
BF, F32 = jnp.bfloat16, jnp.float32

FIRST = ((0, 0), (0, 1), (1, 0))
SECOND = ((1, 1),)
TILES_PER_STEP = 16


def window_kernel(seen_hbm, start_ref, taps_ref, echo_ref, first_ref, second_ref, base_ref, band_ref, seen_ref, sem):
    step = pl.program_id(0)
    members = base_ref.shape[0]
    planes = base_ref.shape[1]
    fetch = pltpu.make_async_copy(seen_hbm, seen_ref, sem)

    @pl.when(step == 0)
    def _():
        fetch.start()
        taps = taps_ref[...].astype(F32)
        offset = lax.broadcasted_iota(jnp.int32, (640, 128), 0) - 4 * lax.broadcasted_iota(jnp.int32, (640, 128), 1)
        for c in range(2):
            band = jnp.zeros((640, 128), F32)
            for k in range(taps.shape[1]):
                band = jnp.where(offset == k, taps[c : c + 1, k : k + 1], band)
            band_ref[:, 128 * c : 128 * c + 128] = band.astype(BF)

    @pl.when(step < members)
    def _():
        rows = []
        for plane in range(planes):
            x = echo_ref[0, plane]
            x = jnp.concatenate([x, jnp.zeros((x.shape[0], 128), x.dtype)], axis=1)
            for j in range(4):
                rows.append(x[:, 512 * j : 512 * j + 640])
        out = jnp.dot(jnp.concatenate(rows, axis=0), band_ref[...], preferred_element_type=F32)
        out = out.astype(BF).astype(F32)
        for plane in range(planes):
            for j in range(4):
                r = 64 * (4 * plane + j)
                base_ref[step, plane, j, 0:64, :] = out[r : r + 64, 0:128]
                base_ref[step, plane, j, 64:128, :] = out[r : r + 64, 128:256]

    @pl.when(step == members)
    def _():
        fetch.wait()

    @pl.when(step >= members)
    def _():
        lane = lax.broadcasted_iota(jnp.int32, (128, 128), 1)
        me = lax.axis_index(AXES)
        for i in range(TILES_PER_STEP):
            tile = (step - members) * TILES_PER_STEP + i
            for ref, units in ((first_ref, FIRST), (second_ref, SECOND)):
                for k, (slot, plane) in enumerate(units):
                    seen = seen_ref[tile * 2 + slot, me]
                    member = jnp.maximum(seen, 0)
                    start = start_ref[plane * 2 + slot, tile]
                    block = start // 128
                    shift = start - 128 * block
                    here = base_ref[member, plane, block]
                    after = base_ref[member, plane, jnp.minimum(block + 1, 3)]
                    both = jnp.where(lane >= shift, here, after)
                    out = pltpu.roll(both, (128 - shift) & 127, 1)
                    ref[i, k] = jnp.where(seen >= 0, out, 0.0).astype(BF)


def make_windows(echoes, taps, seen, starts):
    members, planes, frames, samples = echoes.shape
    tiles = starts.shape[1]
    steps = members + tiles // TILES_PER_STEP
    last = members - 1

    def out_map(i):
        return (jnp.maximum(i - members, 0), 0, 0, 0)

    return pl.pallas_call(
        window_kernel,
        grid=(steps,),
        in_specs=[
            pl.BlockSpec(memory_space=pl.ANY),
            pl.BlockSpec(memory_space=pltpu.SMEM),
            pl.BlockSpec(taps.shape, lambda i: (0, 0)),
            pl.BlockSpec((1, planes, frames, samples), lambda i: (jnp.minimum(i, last), 0, 0, 0)),
        ],
        out_specs=[pl.BlockSpec((TILES_PER_STEP, len(units), 128, 128), out_map) for units in (FIRST, SECOND)],
        scratch_shapes=[
            pltpu.VMEM((members, planes, 4, 128, 128), F32),
            pltpu.VMEM((640, 256), BF),
            pltpu.SMEM(seen.shape, jnp.int32),
            pltpu.SemaphoreType.DMA,
        ],
        out_shape=[jax.ShapeDtypeStruct((tiles, len(units), 128, 128), BF) for units in (FIRST, SECOND)],
        compiler_params=pltpu.CompilerParams(vmem_limit_bytes=60 * 2**20),
        cost_estimate=pl.CostEstimate(flops=2 * 10**9, bytes_accessed=20 * 2**20, transcendentals=0),
        name="windows",
    )(seen, starts, taps, echoes)


def weights(lag):
    lag = jnp.broadcast_to(lag.astype(F32) * 0.25 - 64.0, (16, lag.shape[1])).astype(BF)
    iota = lax.broadcasted_iota(jnp.int32, (16, 128), 0).astype(F32)
    one, zero = jnp.ones((), BF), jnp.zeros((), BF)
    columns = []
    for c in range(lag.shape[1] // 128):
        d = lag[:, 128 * c : 128 * c + 128]
        columns.append(
            jnp.concatenate(
                [jnp.maximum(one - jnp.abs(d - (iota + (16.0 * w - 64.0)).astype(BF)), zero) for w in range(8)], axis=0
            )
        )
    return jnp.concatenate(columns, axis=1)


def accumulate(units, group, windows_ref, lag_ref, acc_ref):
    todo = [(b, k) for b in range(group) for k in range(len(units))]
    for at in range(0, len(todo), 2):
        pair = todo[at : at + 2]
        lhs = jnp.concatenate([windows_ref[b, k] for b, k in pair], axis=1)
        for v in range(0, acc_ref.shape[1], 256):
            rhs = []
            for b, k in pair:
                slot, plane = units[k]
                rhs.append(weights(lag_ref[plane, b, slot : slot + 1, v : v + 256]))
            acc_ref[:, v : v + 256] += jnp.dot(lhs, jnp.concatenate(rhs, axis=0), preferred_element_type=F32)


def first_beam_kernel(units, group, lag_ref, windows_ref, out_ref):
    @pl.when(pl.program_id(0) == 0)
    def _():
        out_ref[...] = jnp.zeros_like(out_ref)

    accumulate(units, group, windows_ref, lag_ref, out_ref)


def second_beam_kernel(units, group, gain_ref, lag_ref, windows_ref, before_ref, out_ref, gram_ref):
    @pl.when(pl.program_id(0) == 0)
    def _():
        out_ref[...] = before_ref[...]

    accumulate(units, group, windows_ref, lag_ref, out_ref)

    @pl.when(pl.program_id(0) == pl.num_programs(0) - 1)
    def _():
        beam = out_ref[...] * gain_ref[0]
        out_ref[...] = beam
        gram_ref[...] = lax.dot_general(
            beam, beam, (((1,), (1,)), ((), ())), precision=lax.Precision.HIGHEST, preferred_element_type=F32
        )


def beam_call(units, group, lags, windows, gain=None, before=None):
    planes, blocks, slots, voxels = lags.shape
    body = second_beam_kernel if before is not None else first_beam_kernel
    in_specs = [
        pl.BlockSpec((planes, group, slots, voxels), lambda i: (0, i, 0, 0)),
        pl.BlockSpec((group, len(units), 128, 128), lambda i: (i, 0, 0, 0)),
    ]
    args = [lags, windows]
    whole = pl.BlockSpec((128, voxels), lambda i: (0, 0))
    out_shape = [jax.ShapeDtypeStruct((128, voxels), F32)]
    out_specs = [whole]
    if before is not None:
        in_specs = [pl.BlockSpec(memory_space=pltpu.SMEM)] + in_specs + [whole]
        args = [gain] + args + [before]
        out_shape.append(jax.ShapeDtypeStruct((128, 128), F32))
        out_specs.append(pl.BlockSpec((128, 128), lambda i: (0, 0)))

    def kernel(*refs):
        body(units, group, *refs)

    return pl.pallas_call(
        kernel,
        grid=(blocks // group,),
        in_specs=in_specs,
        out_specs=out_specs,
        out_shape=out_shape,
        compiler_params=pltpu.CompilerParams(vmem_limit_bytes=48 * 2**20),
        cost_estimate=pl.CostEstimate(
            flops=2 * 128 * voxels * 128 * blocks * len(units),
            bytes_accessed=blocks * len(units) * (128 * 256 + 8 * voxels),
            transcendentals=0,
        ),
        name="beam",
    )(*args)


def invert(a):
    n = a.shape[0]
    lane = lax.broadcasted_iota(jnp.int32, (n, n), 1)
    lane_row = lane[:1]
    sub = lax.broadcasted_iota(jnp.int32, (8, n), 0)
    for k in range(0, n, 2):
        row0, row1 = a[k : k + 1, :], a[k + 1 : k + 2, :]
        col0 = jnp.broadcast_to(a[:, k : k + 1], (n, n))
        col1 = jnp.broadcast_to(a[:, k + 1 : k + 2], (n, n))
        p00, p01 = col0[k : k + 1], col1[k : k + 1]
        p10, p11 = col0[k + 1 : k + 2], col1[k + 1 : k + 2]
        over = 1.0 / (p00 * p11 - p01 * p10)
        i00, i01, i10, i11 = p11 * over, -p01 * over, -p10 * over, p00 * over
        new0 = jnp.where(lane_row == k, i00, jnp.where(lane_row == k + 1, i01, i00 * row0 + i01 * row1))
        new1 = jnp.where(lane_row == k, i10, jnp.where(lane_row == k + 1, i11, i10 * row0 + i11 * row1))
        a = jnp.where((lane == k) | (lane == k + 1), 0.0, a) - col0 * new0 - col1 * new1
        g = k // 8 * 8
        fixed = jnp.where(sub == k - g, new0, jnp.where(sub == k + 1 - g, new1, a[g : g + 8]))
        a = jnp.concatenate([part for part in (a[:g], fixed, a[g + 8 :]) if part.shape[0]], axis=0)
    return a


def power_kernel(samples, gram_ref, beam_ref, out_ref):
    n = gram_ref.shape[0]
    gram = gram_ref[...]
    eye = lax.broadcasted_iota(jnp.int32, (n, n), 0) == lax.broadcasted_iota(jnp.int32, (n, n), 1)
    energy = jnp.sum(jnp.where(eye, gram, 0.0), keepdims=True)
    correlation = gram * (n / energy)
    filter_matrix = damping * invert(correlation + jnp.where(eye, damping, 0.0))
    filtered = lax.dot_general(
        filter_matrix,
        beam_ref[...],
        (((0,), (0,)), ((), ())),
        precision=lax.Precision.HIGHEST,
        preferred_element_type=F32,
    ) / jnp.sqrt(energy / samples)
    out_ref[...] = jnp.log(jnp.sum(filtered * filtered, axis=0, keepdims=True) / n + 1e-06)


def doppler_power(samples, gram, beam):
    def kernel(*refs):
        power_kernel(samples, *refs)

    return pl.pallas_call(
        kernel,
        out_shape=jax.ShapeDtypeStruct((1, beam.shape[1]), F32),
        compiler_params=pltpu.CompilerParams(vmem_limit_bytes=48 * 2**20),
        name="power",
    )(gram, beam)


def exchange_sum(x):
    for axis, digits in (("elem", (1,)), ("elem", (2, 4, 6)), ("vox", (1, 2, 3)), ("vox", (4, 8, 12))):
        size = lax.axis_size(axis)
        parts = [lax.ppermute(x, axis, [(i, i ^ k) for i in range(size)]) for k in digits]
        for part in parts:
            x = x + part
    return x


def shards(echoes, filter_taps, visible, window_start, delays, tile_gain):
    members, planes, frames, samples = echoes.shape
    channels = 2 * frames
    device_count = lax.axis_size("elem") * lax.axis_size("vox")
    voxels = delays.shape[-1]

    seen = jnp.transpose(visible, (0, 2, 1)).reshape(-1, visible.shape[1])
    starts = jnp.transpose(window_start[:, :, 0, :], (0, 2, 1)).reshape(-1, window_start.shape[1])
    first, second = make_windows(echoes, filter_taps, seen, starts)

    first = lax.all_to_all(first, AXES, split_axis=0, concat_axis=0, tiled=True)
    second = lax.all_to_all(second, AXES, split_axis=0, concat_axis=0, tiled=True)
    lags = delays[:, 0]
    (partial,) = beam_call(FIRST, 4, lags, first)
    beam, local_gram = beam_call(SECOND, 8, lags, second, tile_gain, partial)

    frame_gram = exchange_sum(local_gram)
    return doppler_power(channels * device_count * voxels, frame_gram, beam)


def solution(mesh):
    placed = (
        P(AXES, None, None, None),
        P(),
        P(),
        P(None, None, AXES, None),
        P(None, AXES, None, None, None),
        P(AXES),
    )
    return jax.shard_map(
        shards, mesh=mesh, in_specs=placed, out_specs=P(AXES, None), check_vma=False
    )
```

```python
import jax
import jax.numpy as jnp
from jax import lax
from jax.experimental import pallas as pl
from jax.experimental.pallas import tpu as pltpu
from jax.sharding import PartitionSpec as P

W = 128
damping = 0.5
AXES = ("elem", "vox")
BF, F32 = jnp.bfloat16, jnp.float32

FIRST = ((0, 0), (0, 1), (1, 0))
SECOND = ((1, 1),)
TILES_PER_STEP = 32
MEMBERS_PER_STEP = 2
LIST_GROUP = 8


def window_kernel(seen_hbm, start_ref, taps_ref, echo_ref, first_ref, second_ref, base_ref, band_ref, seen_ref, sem):
    step = pl.program_id(0)
    demod_steps = base_ref.shape[0] // MEMBERS_PER_STEP
    planes = base_ref.shape[1]
    fetch = pltpu.make_async_copy(seen_hbm, seen_ref, sem)

    @pl.when(step == 0)
    def _():
        fetch.start()
        taps = taps_ref[...].astype(F32)
        offset = lax.broadcasted_iota(jnp.int32, (640, 128), 0) - 4 * lax.broadcasted_iota(jnp.int32, (640, 128), 1)
        for c in range(2):
            band = jnp.zeros((640, 128), F32)
            for k in range(taps.shape[1]):
                band = jnp.where(offset == k, taps[c : c + 1, k : k + 1], band)
            band_ref[:, 128 * c : 128 * c + 128] = band.astype(BF)

    @pl.when(step < demod_steps)
    def _():
        for m in range(MEMBERS_PER_STEP):
            rows = []
            for plane in range(planes):
                x = echo_ref[m, plane]
                x = jnp.concatenate([x, jnp.zeros((x.shape[0], 128), x.dtype)], axis=1)
                for j in range(4):
                    rows.append(x[:, 512 * j : 512 * j + 640])
            out = jnp.dot(jnp.concatenate(rows, axis=0), band_ref[...], preferred_element_type=F32)
            out = out.astype(BF).astype(F32)
            for plane in range(planes):
                for j in range(4):
                    r = 64 * (4 * plane + j)
                    base_ref[MEMBERS_PER_STEP * step + m, plane, j, 0:64, :] = out[r : r + 64, 0:128]
                    base_ref[MEMBERS_PER_STEP * step + m, plane, j, 64:128, :] = out[r : r + 64, 128:256]

    @pl.when(step == demod_steps)
    def _():
        fetch.wait()

    @pl.when(step >= demod_steps)
    def _():
        lane = lax.broadcasted_iota(jnp.int32, (128, 128), 1)
        me = lax.axis_index(AXES)
        for i in range(TILES_PER_STEP):
            tile = (step - demod_steps) * TILES_PER_STEP + i
            seen0 = seen_ref[tile * 2, me]
            seen1 = seen_ref[tile * 2 + 1, me]
            keep = seen0 >= 0
            seen_at = (jnp.where(keep, seen0, seen1), jnp.where(keep, seen1, -1))
            for ref, units in ((first_ref, FIRST), (second_ref, SECOND)):
                for k, (place, plane) in enumerate(units):
                    seen = seen_at[place]
                    start = start_ref[plane * 2 + 1, tile]
                    if place == 0:
                        start = jnp.where(keep, start_ref[plane * 2, tile], start)
                    member = jnp.maximum(seen, 0)
                    block = start // 128
                    shift = start - 128 * block
                    here = base_ref[member, plane, block]
                    after = base_ref[member, plane, jnp.minimum(block + 1, 3)]
                    both = jnp.where(lane >= shift, here, after)
                    out = pltpu.roll(both, (128 - shift) & 127, 1)
                    ref[i, k] = jnp.where(seen >= 0, out, 0.0).astype(BF)


def make_windows(echoes, taps, seen, starts):
    members, planes, frames, samples = echoes.shape
    tiles = starts.shape[1]
    demod_steps = members // MEMBERS_PER_STEP

    def out_map(i):
        return (jnp.maximum(i - demod_steps, 0), 0, 0, 0)

    return pl.pallas_call(
        window_kernel,
        grid=(demod_steps + tiles // TILES_PER_STEP,),
        in_specs=[
            pl.BlockSpec(memory_space=pl.ANY),
            pl.BlockSpec(memory_space=pltpu.SMEM),
            pl.BlockSpec(taps.shape, lambda i: (0, 0)),
            pl.BlockSpec(
                (MEMBERS_PER_STEP, planes, frames, samples), lambda i: (jnp.minimum(i, demod_steps - 1), 0, 0, 0)
            ),
        ],
        out_specs=[pl.BlockSpec((TILES_PER_STEP, len(units), 128, 128), out_map) for units in (FIRST, SECOND)],
        scratch_shapes=[
            pltpu.VMEM((members, planes, 4, 128, 128), F32),
            pltpu.VMEM((640, 256), BF),
            pltpu.SMEM(seen.shape, jnp.int32),
            pltpu.SemaphoreType.DMA,
        ],
        out_shape=[jax.ShapeDtypeStruct((tiles, len(units), 128, 128), BF) for units in (FIRST, SECOND)],
        compiler_params=pltpu.CompilerParams(vmem_limit_bytes=60 * 2**20),
        cost_estimate=pl.CostEstimate(flops=2 * 10**9, bytes_accessed=20 * 2**20, transcendentals=0),
        name="windows",
    )(seen, starts, taps, echoes)


def weights(lag):
    lag = jnp.broadcast_to(lag.astype(F32) * 0.25 - 64.0, (16, lag.shape[1])).astype(BF)
    iota = lax.broadcasted_iota(jnp.int32, (16, 128), 0).astype(F32)
    one, zero = jnp.ones((), BF), jnp.zeros((), BF)
    columns = []
    for c in range(lag.shape[1] // 128):
        d = lag[:, 128 * c : 128 * c + 128]
        columns.append(
            jnp.concatenate(
                [jnp.maximum(one - jnp.abs(d - (iota + (16.0 * w - 64.0)).astype(BF)), zero) for w in range(8)], axis=0
            )
        )
    return jnp.concatenate(columns, axis=1)


def add_pieces(pieces, acc_ref):
    for at in range(0, len(pieces), 2):
        pair = pieces[at : at + 2]
        lhs = jnp.concatenate([windows() for windows, lags in pair], axis=1)
        for v in range(0, acc_ref.shape[1], 256):
            rhs = jnp.concatenate([weights(lags(slice(v, v + 256))) for windows, lags in pair], axis=0)
            acc_ref[:, v : v + 256] += jnp.dot(lhs, rhs, preferred_element_type=F32)


def first_beam_kernel(group, swap_ref, lag_ref, windows_ref, out_ref):
    step = pl.program_id(0)

    @pl.when(step == 0)
    def _():
        out_ref[...] = jnp.zeros_like(out_ref)

    def piece(b, k, place, plane):
        def lags(voxels):
            kept = lag_ref[plane, b, place : place + 1, voxels]
            if place == 1:
                return kept
            return jnp.where(swap_ref[step * group + b] == 1, lag_ref[plane, b, 1:2, voxels], kept)

        return (lambda: windows_ref[b, k]), lags

    add_pieces([piece(b, k, *unit) for b in range(group) for k, unit in enumerate(FIRST)], out_ref)


def first_beam(group, swap, lags, windows):
    planes, blocks, slots, voxels = lags.shape
    units = len(FIRST)

    def kernel(*refs):
        first_beam_kernel(group, *refs)

    return pl.pallas_call(
        kernel,
        grid_spec=pltpu.PrefetchScalarGridSpec(
            num_scalar_prefetch=1,
            grid=(blocks // group,),
            in_specs=[
                pl.BlockSpec((planes, group, slots, voxels), lambda i, *_: (0, i, 0, 0)),
                pl.BlockSpec((group, units, 128, 128), lambda i, *_: (i, 0, 0, 0)),
            ],
            out_specs=pl.BlockSpec((128, voxels), lambda i, *_: (0, 0)),
        ),
        out_shape=jax.ShapeDtypeStruct((128, voxels), F32),
        compiler_params=pltpu.CompilerParams(vmem_limit_bytes=48 * 2**20),
        cost_estimate=pl.CostEstimate(
            flops=2 * 128 * voxels * 128 * blocks * units,
            bytes_accessed=blocks * units * (128 * 256 + 8 * voxels),
            transcendentals=0,
        ),
        name="beam",
    )(swap, lags, windows)


def second_beam_kernel(list_ref, gain_ref, lag_ref, *refs):
    window_refs = refs[:LIST_GROUP]
    before_hbm, out_ref, gram_ref, before_ref, sem = refs[LIST_GROUP:]
    step = pl.program_id(0)
    ((place, plane),) = SECOND
    fetch = pltpu.make_async_copy(before_hbm, before_ref, sem)

    @pl.when(step == 0)
    def _():
        fetch.start()
        out_ref[...] = jnp.zeros_like(out_ref)

    @pl.when(step * LIST_GROUP < list_ref[lag_ref.shape[1]])
    def _():
        def piece(j):
            block = list_ref[step * LIST_GROUP + j]
            return (lambda: window_refs[j][0, 0]), (lambda voxels: lag_ref[0, block, place : place + 1, voxels])

        add_pieces([piece(j) for j in range(LIST_GROUP)], out_ref)

    @pl.when(step == pl.num_programs(0) - 1)
    def _():
        fetch.wait()
        beam = (before_ref[...] + out_ref[...]) * gain_ref[0]
        out_ref[...] = beam
        high = beam.astype(BF)
        rest = beam - high.astype(F32)
        middle = rest.astype(BF)
        low = (rest - middle.astype(F32)).astype(BF)
        dims = (((1,), (1,)), ((), ()))
        stacked = jnp.concatenate([high, middle], axis=0)
        main = lax.dot_general(stacked, stacked, dims, preferred_element_type=F32)
        cross = main[:128, 128:] + lax.dot_general(high, low, dims, preferred_element_type=F32)
        gram_ref[...] = main[:128, :128] + (cross + cross.T + main[128:, 128:])


def second_beam(order, gain, lags, windows, before):
    planes, blocks, slots, voxels = lags.shape
    ((place, plane),) = SECOND
    steps = blocks // LIST_GROUP

    def window_spec(j):
        def index(i, order):
            last = jnp.maximum((order[blocks] + LIST_GROUP - 1) // LIST_GROUP - 1, 0)
            return (order[jnp.minimum(i, last) * LIST_GROUP + j], 0, 0, 0)

        return pl.BlockSpec((1, 1, 128, 128), index)

    return pl.pallas_call(
        second_beam_kernel,
        grid_spec=pltpu.PrefetchScalarGridSpec(
            num_scalar_prefetch=1,
            grid=(steps,),
            in_specs=[
                pl.BlockSpec(memory_space=pltpu.SMEM),
                pl.BlockSpec((1, blocks, slots, voxels), lambda i, *_: (plane, 0, 0, 0)),
            ]
            + [window_spec(j) for j in range(LIST_GROUP)]
            + [pl.BlockSpec(memory_space=pl.ANY)],
            out_specs=[
                pl.BlockSpec((128, voxels), lambda i, *_: (0, 0)),
                pl.BlockSpec((128, 128), lambda i, *_: (0, 0)),
            ],
            scratch_shapes=[pltpu.VMEM((128, voxels), F32), pltpu.SemaphoreType.DMA],
        ),
        out_shape=[jax.ShapeDtypeStruct((128, voxels), F32), jax.ShapeDtypeStruct((128, 128), F32)],
        compiler_params=pltpu.CompilerParams(vmem_limit_bytes=48 * 2**20),
        cost_estimate=pl.CostEstimate(
            flops=2 * 128 * voxels * 128 * blocks,
            bytes_accessed=blocks * (128 * 256 + 8 * voxels),
            transcendentals=0,
        ),
        name="beam",
    )(order, gain, lags, *([windows] * LIST_GROUP), before)


def live_order(seen):
    blocks = seen.shape[0]
    swap = ((seen[:, 0] < 0) & (seen[:, 1] >= 0)).astype(jnp.int32)
    key = 1 - ((seen[:, 0] >= 0) & (seen[:, 1] >= 0)).astype(jnp.int32)
    ids = jnp.arange(blocks, dtype=jnp.int32)
    key = key * blocks + ids
    rank = jnp.sum((key[None, :] < key[:, None]).astype(jnp.int32), axis=1)
    order = jnp.sum(jnp.where(rank[None, :] == ids[:, None], ids[None, :], 0), axis=1)
    count = jnp.sum((key < blocks).astype(jnp.int32), keepdims=True)
    return swap, jnp.concatenate([order, count])


def product2(x, y):
    return [[x[i][0] * y[0][j] + x[i][1] * y[1][j] for j in range(2)] for i in range(2)]


def inverse2(x):
    over = 1.0 / (x[0][0] * x[1][1] - x[0][1] * x[1][0])
    return [[x[1][1] * over, -x[0][1] * over], [-x[1][0] * over, x[0][0] * over]]


def inverse4(p):
    e, f, g, h = ([[p[r + i][c + j] for j in range(2)] for i in range(2)] for r in (0, 2) for c in (0, 2))
    e = inverse2(e)
    ge, ef = product2(g, e), product2(e, f)
    t = product2(g, ef)
    s = inverse2([[h[i][j] - t[i][j] for j in range(2)] for i in range(2)])
    right, left = product2(ef, s), product2(s, ge)
    t = product2(right, ge)
    top = [[e[i][0] + t[i][0], e[i][1] + t[i][1], -right[i][0], -right[i][1]] for i in range(2)]
    return top + [[-left[i][0], -left[i][1], s[i][0], s[i][1]] for i in range(2)]


def invert(a):
    n = a.shape[0]
    lane = lax.broadcasted_iota(jnp.int32, (n, n), 1)
    lane_row = lane[:1]
    sub = lax.broadcasted_iota(jnp.int32, (8, n), 0)
    for k in range(0, n, 4):
        rows = [a[k + i : k + i + 1, :] for i in range(4)]
        cols = [jnp.broadcast_to(a[:, k + i : k + i + 1], (n, n)) for i in range(4)]
        pivot = inverse4([[cols[j][k + i : k + i + 1] for j in range(4)] for i in range(4)])
        new = []
        for i in range(4):
            q = pivot[i]
            row = (q[0] * rows[0] + q[1] * rows[1]) + (q[2] * rows[2] + q[3] * rows[3])
            for j in range(4):
                row = jnp.where(lane_row == k + j, q[j], row)
            new.append(row)
        update = (cols[0] * new[0] + cols[1] * new[1]) + (cols[2] * new[2] + cols[3] * new[3])
        a = jnp.where((lane >= k) & (lane < k + 4), 0.0, a) - update
        g = k // 8 * 8
        fixed = a[g : g + 8]
        for i in range(4):
            fixed = jnp.where(sub == k + i - g, new[i], fixed)
        a = jnp.concatenate([part for part in (a[:g], fixed, a[g + 8 :]) if part.shape[0]], axis=0)
    return a


def power_kernel(samples, gram_ref, beam_ref, out_ref):
    n = gram_ref.shape[0]
    gram = gram_ref[...]
    eye = lax.broadcasted_iota(jnp.int32, (n, n), 0) == lax.broadcasted_iota(jnp.int32, (n, n), 1)
    energy = jnp.sum(jnp.where(eye, gram, 0.0), keepdims=True)
    correlation = gram * (n / energy)
    filter_matrix = damping * invert(correlation + jnp.where(eye, damping, 0.0))
    filtered = lax.dot_general(
        filter_matrix,
        beam_ref[...],
        (((0,), (0,)), ((), ())),
        precision=lax.Precision.HIGHEST,
        preferred_element_type=F32,
    ) / jnp.sqrt(energy / samples)
    out_ref[...] = jnp.log(jnp.sum(filtered * filtered, axis=0, keepdims=True) / n + 1e-06)


def doppler_power(samples, gram, beam):
    def kernel(*refs):
        power_kernel(samples, *refs)

    return pl.pallas_call(
        kernel,
        out_shape=jax.ShapeDtypeStruct((1, beam.shape[1]), F32),
        compiler_params=pltpu.CompilerParams(vmem_limit_bytes=48 * 2**20),
        name="power",
    )(gram, beam)


def exchange_sum(x):
    for axis, digits in (("elem", (1,)), ("elem", (2, 4, 6)), ("vox", (1, 2, 3)), ("vox", (4, 8, 12))):
        size = lax.axis_size(axis)
        parts = [lax.ppermute(x, axis, [(i, i ^ k) for i in range(size)]) for k in digits]
        for part in parts:
            x = x + part
    return x


def shards(echoes, filter_taps, visible, window_start, delays, tile_gain):
    members, planes, frames, samples = echoes.shape
    channels = 2 * frames
    device_count = lax.axis_size("elem") * lax.axis_size("vox")
    voxels = delays.shape[-1]

    seen = jnp.transpose(visible, (0, 2, 1)).reshape(-1, visible.shape[1])
    starts = jnp.transpose(window_start[:, :, 0, :], (0, 2, 1)).reshape(-1, window_start.shape[1])
    first, second = make_windows(echoes, filter_taps, seen, starts)

    first = lax.all_to_all(first, AXES, split_axis=0, concat_axis=0, tiled=True)
    second = lax.all_to_all(second, AXES, split_axis=0, concat_axis=0, tiled=True)
    visible, first = lax.optimization_barrier((visible, first))
    my_seen = lax.dynamic_index_in_dim(visible, lax.axis_index(AXES), 0, keepdims=False)
    swap, order = live_order(my_seen)
    lags = delays[:, 0]
    partial = first_beam(4, swap, lags, first)
    beam, local_gram = second_beam(order, tile_gain, lags, second, partial)

    frame_gram = exchange_sum(local_gram)
    return doppler_power(channels * device_count * voxels, frame_gram, beam)


def solution(mesh):
    placed = (
        P(AXES, None, None, None),
        P(),
        P(),
        P(None, None, AXES, None),
        P(None, AXES, None, None, None),
        P(AXES),
    )
    return jax.shard_map(
        shards, mesh=mesh, in_specs=placed, out_specs=P(AXES, None), check_vma=False
    )
```

```python
import jax
import jax.numpy as jnp
from jax import lax
from jax.experimental import pallas as pl
from jax.experimental.pallas import tpu as pltpu
from jax.sharding import PartitionSpec as P

W = 128
damping = 0.5
AXES = ("elem", "vox")
BF, F32 = jnp.bfloat16, jnp.float32

FIRST = ((0, 0), (0, 1), (1, 0))
SECOND = ((1, 1),)
TILES_PER_STEP = 32
MEMBERS_PER_STEP = 2
LIST_GROUP = 8


def window_kernel(seen_hbm, start_ref, taps_ref, echo_ref, first_ref, second_ref, base_ref, band_ref, seen_ref, sem):
    step = pl.program_id(0)
    demod_steps = base_ref.shape[0] // MEMBERS_PER_STEP
    planes = base_ref.shape[1]
    fetch = pltpu.make_async_copy(seen_hbm, seen_ref, sem)

    @pl.when(step == 0)
    def _():
        fetch.start()
        taps = taps_ref[...].astype(F32)
        offset = lax.broadcasted_iota(jnp.int32, (640, 128), 0) - 4 * lax.broadcasted_iota(jnp.int32, (640, 128), 1)
        for c in range(2):
            band = jnp.zeros((640, 128), F32)
            for k in range(taps.shape[1]):
                band = jnp.where(offset == k, taps[c : c + 1, k : k + 1], band)
            band_ref[:, 128 * c : 128 * c + 128] = band.astype(BF)

    @pl.when(step < demod_steps)
    def _():
        for m in range(MEMBERS_PER_STEP):
            rows = []
            for plane in range(planes):
                x = echo_ref[m, plane]
                x = jnp.concatenate([x, jnp.zeros((x.shape[0], 128), x.dtype)], axis=1)
                for j in range(4):
                    rows.append(x[:, 512 * j : 512 * j + 640])
            out = jnp.dot(jnp.concatenate(rows, axis=0), band_ref[...], preferred_element_type=F32)
            out = out.astype(BF).astype(F32)
            for plane in range(planes):
                for j in range(4):
                    r = 64 * (4 * plane + j)
                    base_ref[MEMBERS_PER_STEP * step + m, plane, j, 0:64, :] = out[r : r + 64, 0:128]
                    base_ref[MEMBERS_PER_STEP * step + m, plane, j, 64:128, :] = out[r : r + 64, 128:256]

    @pl.when(step == demod_steps)
    def _():
        fetch.wait()

    @pl.when(step >= demod_steps)
    def _():
        lane = lax.broadcasted_iota(jnp.int32, (128, 128), 1)
        me = lax.axis_index(AXES)
        for i in range(TILES_PER_STEP):
            tile = (step - demod_steps) * TILES_PER_STEP + i
            seen0 = seen_ref[tile * 2, me]
            seen1 = seen_ref[tile * 2 + 1, me]
            keep = seen0 >= 0
            seen_at = (jnp.where(keep, seen0, seen1), jnp.where(keep, seen1, -1))
            for ref, units in ((first_ref, FIRST), (second_ref, SECOND)):
                for k, (place, plane) in enumerate(units):
                    seen = seen_at[place]
                    start = start_ref[plane * 2 + 1, tile]
                    if place == 0:
                        start = jnp.where(keep, start_ref[plane * 2, tile], start)
                    member = jnp.maximum(seen, 0)
                    block = start // 128
                    shift = start - 128 * block
                    here = base_ref[member, plane, block]
                    after = base_ref[member, plane, jnp.minimum(block + 1, 3)]
                    both = jnp.where(lane >= shift, here, after)
                    out = pltpu.roll(both, (128 - shift) & 127, 1)
                    ref[i, k] = jnp.where(seen >= 0, out, 0.0).astype(BF)


def make_windows(echoes, taps, seen, starts):
    members, planes, frames, samples = echoes.shape
    tiles = starts.shape[1]
    demod_steps = members // MEMBERS_PER_STEP

    def out_map(i):
        return (jnp.maximum(i - demod_steps, 0), 0, 0, 0)

    return pl.pallas_call(
        window_kernel,
        grid=(demod_steps + tiles // TILES_PER_STEP,),
        in_specs=[
            pl.BlockSpec(memory_space=pl.ANY),
            pl.BlockSpec(memory_space=pltpu.SMEM),
            pl.BlockSpec(taps.shape, lambda i: (0, 0)),
            pl.BlockSpec(
                (MEMBERS_PER_STEP, planes, frames, samples), lambda i: (jnp.minimum(i, demod_steps - 1), 0, 0, 0)
            ),
        ],
        out_specs=[pl.BlockSpec((TILES_PER_STEP, len(units), 128, 128), out_map) for units in (FIRST, SECOND)],
        scratch_shapes=[
            pltpu.VMEM((members, planes, 4, 128, 128), F32),
            pltpu.VMEM((640, 256), BF),
            pltpu.SMEM(seen.shape, jnp.int32),
            pltpu.SemaphoreType.DMA,
        ],
        out_shape=[jax.ShapeDtypeStruct((tiles, len(units), 128, 128), BF) for units in (FIRST, SECOND)],
        compiler_params=pltpu.CompilerParams(vmem_limit_bytes=60 * 2**20),
        cost_estimate=pl.CostEstimate(flops=2 * 10**9, bytes_accessed=20 * 2**20, transcendentals=0),
        name="windows",
    )(seen, starts, taps, echoes)


def weights(lag):
    lag = jnp.broadcast_to(lag.astype(F32) * 0.25 - 64.0, (16, lag.shape[1])).astype(BF)
    iota = lax.broadcasted_iota(jnp.int32, (16, 128), 0).astype(F32)
    one, zero = jnp.ones((), BF), jnp.zeros((), BF)
    columns = []
    for c in range(lag.shape[1] // 128):
        d = lag[:, 128 * c : 128 * c + 128]
        columns.append(
            jnp.concatenate(
                [jnp.maximum(one - jnp.abs(d - (iota + (16.0 * w - 64.0)).astype(BF)), zero) for w in range(8)], axis=0
            )
        )
    return jnp.concatenate(columns, axis=1)


def add_pieces(pieces, acc_ref):
    for at in range(0, len(pieces), 2):
        pair = pieces[at : at + 2]
        lhs = jnp.concatenate([windows() for windows, lags in pair], axis=1)
        for v in range(0, acc_ref.shape[1], 256):
            rhs = jnp.concatenate([weights(lags(slice(v, v + 256))) for windows, lags in pair], axis=0)
            acc_ref[:, v : v + 256] += jnp.dot(lhs, rhs, preferred_element_type=F32)


def first_beam_kernel(group, swap_ref, lag_ref, windows_ref, out_ref):
    step = pl.program_id(0)

    @pl.when(step == 0)
    def _():
        out_ref[...] = jnp.zeros_like(out_ref)

    def piece(b, k, place, plane):
        def lags(voxels):
            kept = lag_ref[plane, b, place : place + 1, voxels]
            if place == 1:
                return kept
            return jnp.where(swap_ref[step * group + b] == 1, lag_ref[plane, b, 1:2, voxels], kept)

        return (lambda: windows_ref[b, k]), lags

    add_pieces([piece(b, k, *unit) for b in range(group) for k, unit in enumerate(FIRST)], out_ref)


def first_beam(group, swap, lags, windows):
    planes, blocks, slots, voxels = lags.shape
    units = len(FIRST)

    def kernel(*refs):
        first_beam_kernel(group, *refs)

    return pl.pallas_call(
        kernel,
        grid_spec=pltpu.PrefetchScalarGridSpec(
            num_scalar_prefetch=1,
            grid=(blocks // group,),
            in_specs=[
                pl.BlockSpec((planes, group, slots, voxels), lambda i, *_: (0, i, 0, 0)),
                pl.BlockSpec((group, units, 128, 128), lambda i, *_: (i, 0, 0, 0)),
            ],
            out_specs=pl.BlockSpec((128, voxels), lambda i, *_: (0, 0)),
        ),
        out_shape=jax.ShapeDtypeStruct((128, voxels), F32),
        compiler_params=pltpu.CompilerParams(vmem_limit_bytes=62_000_000),
        cost_estimate=pl.CostEstimate(
            flops=2 * 128 * voxels * 128 * blocks * units,
            bytes_accessed=blocks * units * (128 * 256 + 8 * voxels),
            transcendentals=0,
        ),
        name="beam",
    )(swap, lags, windows)


def second_beam_kernel(
    list_ref, gain_ref, lag_ref, before_hbm, windows_hbm, out_ref, gram_ref, before_ref, held_ref, before_sem, sems
):
    ((place, plane),) = SECOND
    count = list_ref[lag_ref.shape[1]]
    groups = (count + LIST_GROUP - 1) // LIST_GROUP

    def fetches(group, half):
        return [
            pltpu.make_async_copy(
                windows_hbm.at[list_ref[group * LIST_GROUP + j], 0], held_ref.at[half, j], sems.at[half, j]
            )
            for j in range(LIST_GROUP)
        ]

    @pl.when(groups > 0)
    def _():
        for copy in fetches(0, 0):
            copy.start()

    before = pltpu.make_async_copy(before_hbm, before_ref, before_sem)
    before.start()
    out_ref[...] = jnp.zeros_like(out_ref)

    def one_group(group, carry):
        half = lax.rem(group, 2)

        @pl.when(group + 1 < groups)
        def _():
            for copy in fetches(group + 1, 1 - half):
                copy.start()

        for copy in fetches(group, half):
            copy.wait()

        def piece(j):
            block = list_ref[group * LIST_GROUP + j]
            return (lambda: held_ref[half, j]), (lambda voxels: lag_ref[plane, block, place : place + 1, voxels])

        add_pieces([piece(j) for j in range(LIST_GROUP)], out_ref)
        return carry

    lax.fori_loop(0, groups, one_group, 0)

    before.wait()
    beam = (before_ref[...] + out_ref[...]) * gain_ref[0]
    out_ref[...] = beam
    high = beam.astype(BF)
    rest = beam - high.astype(F32)
    middle = rest.astype(BF)
    low = (rest - middle.astype(F32)).astype(BF)
    dims = (((1,), (1,)), ((), ()))
    stacked = jnp.concatenate([high, middle], axis=0)
    main = lax.dot_general(stacked, stacked, dims, preferred_element_type=F32)
    cross = main[:128, 128:] + lax.dot_general(high, low, dims, preferred_element_type=F32)
    gram_ref[...] = main[:128, :128] + (cross + cross.T + main[128:, 128:])


def second_beam(order, gain, lags, windows, before):
    planes, blocks, slots, voxels = lags.shape
    smem, vmem = pl.BlockSpec(memory_space=pltpu.SMEM), pl.BlockSpec(memory_space=pltpu.VMEM)
    return pl.pallas_call(
        second_beam_kernel,
        in_specs=[smem, smem, vmem] + [pl.BlockSpec(memory_space=pltpu.HBM)] * 2,
        out_specs=[vmem, vmem],
        out_shape=[jax.ShapeDtypeStruct((128, voxels), F32), jax.ShapeDtypeStruct((128, 128), F32)],
        scratch_shapes=[
            pltpu.VMEM((128, voxels), F32),
            pltpu.VMEM((2, LIST_GROUP, 128, 128), BF),
            pltpu.SemaphoreType.DMA,
            pltpu.SemaphoreType.DMA((2, LIST_GROUP)),
        ],
        compiler_params=pltpu.CompilerParams(vmem_limit_bytes=40 * 2**20),
        cost_estimate=pl.CostEstimate(
            flops=2 * 128 * voxels * 128 * blocks,
            bytes_accessed=blocks * (128 * 256 + 8 * voxels),
            transcendentals=0,
        ),
        name="beam",
    )(order, gain, lags, before, windows)


def live_order(seen):
    blocks = seen.shape[0]
    swap = ((seen[:, 0] < 0) & (seen[:, 1] >= 0)).astype(jnp.int32)
    key = 1 - ((seen[:, 0] >= 0) & (seen[:, 1] >= 0)).astype(jnp.int32)
    ids = jnp.arange(blocks, dtype=jnp.int32)
    key = key * blocks + ids
    rank = jnp.sum((key[None, :] < key[:, None]).astype(jnp.int32), axis=1)
    order = jnp.sum(jnp.where(rank[None, :] == ids[:, None], ids[None, :], 0), axis=1)
    count = jnp.sum((key < blocks).astype(jnp.int32), keepdims=True)
    return swap, jnp.concatenate([order, count])


def product2(x, y):
    return [[x[i][0] * y[0][j] + x[i][1] * y[1][j] for j in range(2)] for i in range(2)]


def inverse2(x):
    over = 1.0 / (x[0][0] * x[1][1] - x[0][1] * x[1][0])
    return [[x[1][1] * over, -x[0][1] * over], [-x[1][0] * over, x[0][0] * over]]


def inverse4(p):
    e, f, g, h = ([[p[r + i][c + j] for j in range(2)] for i in range(2)] for r in (0, 2) for c in (0, 2))
    e = inverse2(e)
    ge, ef = product2(g, e), product2(e, f)
    t = product2(g, ef)
    s = inverse2([[h[i][j] - t[i][j] for j in range(2)] for i in range(2)])
    right, left = product2(ef, s), product2(s, ge)
    t = product2(right, ge)
    top = [[e[i][0] + t[i][0], e[i][1] + t[i][1], -right[i][0], -right[i][1]] for i in range(2)]
    return top + [[-left[i][0], -left[i][1], s[i][0], s[i][1]] for i in range(2)]


def invert(a):
    n = a.shape[0]
    lane = lax.broadcasted_iota(jnp.int32, (n, n), 1)
    lane_row = lane[:1]
    sub = lax.broadcasted_iota(jnp.int32, (8, n), 0)
    for k in range(0, n, 4):
        rows = [a[k + i : k + i + 1, :] for i in range(4)]
        cols = [jnp.broadcast_to(a[:, k + i : k + i + 1], (n, n)) for i in range(4)]
        pivot = inverse4([[cols[j][k + i : k + i + 1] for j in range(4)] for i in range(4)])
        new = []
        for i in range(4):
            q = pivot[i]
            row = (q[0] * rows[0] + q[1] * rows[1]) + (q[2] * rows[2] + q[3] * rows[3])
            for j in range(4):
                row = jnp.where(lane_row == k + j, q[j], row)
            new.append(row)
        update = (cols[0] * new[0] + cols[1] * new[1]) + (cols[2] * new[2] + cols[3] * new[3])
        a = jnp.where((lane >= k) & (lane < k + 4), 0.0, a) - update
        g = k // 8 * 8
        fixed = a[g : g + 8]
        for i in range(4):
            fixed = jnp.where(sub == k + i - g, new[i], fixed)
        a = jnp.concatenate([part for part in (a[:g], fixed, a[g + 8 :]) if part.shape[0]], axis=0)
    return a


def power_kernel(samples, gram_ref, beam_ref, out_ref):
    n = gram_ref.shape[0]
    gram = gram_ref[...]
    eye = lax.broadcasted_iota(jnp.int32, (n, n), 0) == lax.broadcasted_iota(jnp.int32, (n, n), 1)
    energy = jnp.sum(jnp.where(eye, gram, 0.0), keepdims=True)
    correlation = gram * (n / energy)
    filter_matrix = damping * invert(correlation + jnp.where(eye, damping, 0.0))
    filtered = lax.dot_general(
        filter_matrix,
        beam_ref[...],
        (((0,), (0,)), ((), ())),
        precision=lax.Precision.HIGHEST,
        preferred_element_type=F32,
    ) / jnp.sqrt(energy / samples)
    out_ref[...] = jnp.log(jnp.sum(filtered * filtered, axis=0, keepdims=True) / n + 1e-06)


def doppler_power(samples, gram, beam):
    def kernel(*refs):
        power_kernel(samples, *refs)

    return pl.pallas_call(
        kernel,
        out_shape=jax.ShapeDtypeStruct((1, beam.shape[1]), F32),
        compiler_params=pltpu.CompilerParams(vmem_limit_bytes=48 * 2**20),
        name="power",
    )(gram, beam)


def exchange_sum(x):
    for axis, digits in (("elem", (1,)), ("elem", (2, 4, 6)), ("vox", (1, 2, 3)), ("vox", (4, 8, 12))):
        size = lax.axis_size(axis)
        parts = [lax.ppermute(x, axis, [(i, i ^ k) for i in range(size)]) for k in digits]
        for part in parts:
            x = x + part
    return x


def shards(echoes, filter_taps, visible, window_start, delays, tile_gain):
    members, planes, frames, samples = echoes.shape
    channels = 2 * frames
    device_count = lax.axis_size("elem") * lax.axis_size("vox")
    voxels = delays.shape[-1]

    seen = jnp.transpose(visible, (0, 2, 1)).reshape(-1, visible.shape[1])
    starts = jnp.transpose(window_start[:, :, 0, :], (0, 2, 1)).reshape(-1, window_start.shape[1])
    first, second = make_windows(echoes, filter_taps, seen, starts)

    first = lax.all_to_all(first, AXES, split_axis=0, concat_axis=0, tiled=True)
    second = lax.all_to_all(second, AXES, split_axis=0, concat_axis=0, tiled=True)
    visible, first = lax.optimization_barrier((visible, first))
    my_seen = lax.dynamic_index_in_dim(visible, lax.axis_index(AXES), 0, keepdims=False)
    swap, order = live_order(my_seen)
    lags = delays[:, 0]
    partial = first_beam(4, swap, lags, first)
    beam, local_gram = second_beam(order, tile_gain, lags, second, partial)

    frame_gram = exchange_sum(local_gram)
    return doppler_power(channels * device_count * voxels, frame_gram, beam)


def solution(mesh):
    placed = (
        P(AXES, None, None, None),
        P(),
        P(),
        P(None, None, AXES, None),
        P(None, AXES, None, None, None),
        P(AXES),
    )
    return jax.shard_map(
        shards, mesh=mesh, in_specs=placed, out_specs=P(AXES, None), check_vma=False
    )
```

```python
import jax
import jax.numpy as jnp
from jax import lax
from jax.experimental import pallas as pl
from jax.experimental.pallas import tpu as pltpu
from jax.sharding import PartitionSpec as P

W = 128
damping = 0.5
AXES = ("elem", "vox")
BF, F32 = jnp.bfloat16, jnp.float32

FIRST = ((0, 0), (0, 1), (1, 0))
SECOND = ((1, 1),)
TILES_PER_STEP = 32
MEMBERS_PER_STEP = 4
LIST_GROUP = 8


def window_kernel(seen_hbm, start_ref, taps_ref, echo_ref, first_ref, second_ref, base_ref, band_ref, seen_ref, sem):
    step = pl.program_id(0)
    planes = echo_ref.shape[1]
    zeros = base_ref.shape[0] - 2
    demod_steps = zeros // (4 * planes * MEMBERS_PER_STEP)
    fetch = pltpu.make_async_copy(seen_hbm, seen_ref, sem)

    @pl.when(step == 0)
    def _():
        fetch.start()
        base_ref[zeros:, :, :] = jnp.zeros((2, 128, 128), F32)
        taps = taps_ref[...].astype(F32)
        offset = lax.broadcasted_iota(jnp.int32, (640, 128), 0) - 4 * lax.broadcasted_iota(jnp.int32, (640, 128), 1)
        for c in range(2):
            band = jnp.zeros((640, 128), F32)
            for k in range(taps.shape[1]):
                band = jnp.where(offset == k, taps[c : c + 1, k : k + 1], band)
            band_ref[:, 128 * c : 128 * c + 128] = band.astype(BF)

    @pl.when(step < demod_steps)
    def _():
        for m in range(MEMBERS_PER_STEP):
            rows = []
            for plane in range(planes):
                x = echo_ref[m, plane]
                x = jnp.concatenate([x, jnp.zeros((x.shape[0], 128), x.dtype)], axis=1)
                for j in range(4):
                    rows.append(x[:, 512 * j : 512 * j + 640])
            out = jnp.dot(jnp.concatenate(rows, axis=0), band_ref[...], preferred_element_type=F32)
            out = out.astype(BF).astype(F32)
            for plane in range(planes):
                for j in range(4):
                    r = 64 * (4 * plane + j)
                    part = (MEMBERS_PER_STEP * step + m) * (4 * planes) + (4 * plane + j)
                    base_ref[part, 0:64, :] = out[r : r + 64, 0:128]
                    base_ref[part, 64:128, :] = out[r : r + 64, 128:256]

    @pl.when(step == demod_steps)
    def _():
        fetch.wait()

    @pl.when(step >= demod_steps)
    def _():
        lane = lax.broadcasted_iota(jnp.int32, (128, 128), 1)
        me = lax.axis_index(AXES)
        for i in range(TILES_PER_STEP):
            tile = (step - demod_steps) * TILES_PER_STEP + i
            seen0 = seen_ref[tile * 2, me]
            seen1 = seen_ref[tile * 2 + 1, me]
            keep = seen0 >= 0
            seen_at = (jnp.where(keep, seen0, seen1), jnp.where(keep, seen1, -1))
            for ref, units in ((first_ref, FIRST), (second_ref, SECOND)):
                for k, (place, plane) in enumerate(units):
                    seen = seen_at[place]
                    start = start_ref[plane * 2 + 1, tile]
                    if place == 0:
                        start = jnp.where(keep, start_ref[plane * 2, tile], start)
                    part = seen * (4 * planes) + (4 * plane + lax.shift_right_logical(start, 7))
                    part = jnp.where(seen >= 0, part, zeros)
                    both = jnp.where(lane >= (start & 127), base_ref[part], base_ref[part + 1])
                    out = pltpu.roll(both, (0 - start) & 127, 1)
                    ref[i, k] = out.astype(BF)


def make_windows(echoes, taps, seen, starts):
    members, planes, frames, samples = echoes.shape
    tiles = starts.shape[1]
    demod_steps = members // MEMBERS_PER_STEP

    def out_map(i):
        return (jnp.maximum(i - demod_steps, 0), 0, 0, 0)

    return pl.pallas_call(
        window_kernel,
        grid=(demod_steps + tiles // TILES_PER_STEP,),
        in_specs=[
            pl.BlockSpec(memory_space=pl.ANY),
            pl.BlockSpec(memory_space=pltpu.SMEM),
            pl.BlockSpec(taps.shape, lambda i: (0, 0)),
            pl.BlockSpec(
                (MEMBERS_PER_STEP, planes, frames, samples), lambda i: (jnp.minimum(i, demod_steps - 1), 0, 0, 0)
            ),
        ],
        out_specs=[pl.BlockSpec((TILES_PER_STEP, len(units), 128, 128), out_map) for units in (FIRST, SECOND)],
        scratch_shapes=[
            pltpu.VMEM((4 * members * planes + 2, 128, 128), F32),
            pltpu.VMEM((640, 256), BF),
            pltpu.SMEM(seen.shape, jnp.int32),
            pltpu.SemaphoreType.DMA,
        ],
        out_shape=[jax.ShapeDtypeStruct((tiles, len(units), 128, 128), BF) for units in (FIRST, SECOND)],
        compiler_params=pltpu.CompilerParams(vmem_limit_bytes=60 * 2**20),
        cost_estimate=pl.CostEstimate(flops=2 * 10**9, bytes_accessed=20 * 2**20, transcendentals=0),
        name="windows",
    )(seen, starts, taps, echoes)


def weights(lag):
    lag = jnp.broadcast_to(lag.astype(F32) * 0.25 - 64.0, (16, lag.shape[1])).astype(BF)
    iota = lax.broadcasted_iota(jnp.int32, (16, 128), 0).astype(F32)
    one, zero = jnp.ones((), BF), jnp.zeros((), BF)
    columns = []
    for c in range(lag.shape[1] // 128):
        d = lag[:, 128 * c : 128 * c + 128]
        columns.append(
            jnp.concatenate(
                [jnp.maximum(one - jnp.abs(d - (iota + (16.0 * w - 64.0)).astype(BF)), zero) for w in range(8)], axis=0
            )
        )
    return jnp.concatenate(columns, axis=1)


def add_pieces(pieces, acc_ref):
    for at in range(0, len(pieces), 2):
        pair = pieces[at : at + 2]
        lhs = jnp.concatenate([windows() for windows, lags in pair], axis=1)
        for v in range(0, acc_ref.shape[1], 256):
            rhs = jnp.concatenate([weights(lags(slice(v, v + 256))) for windows, lags in pair], axis=0)
            acc_ref[:, v : v + 256] += jnp.dot(lhs, rhs, preferred_element_type=F32)


def first_beam_kernel(group, swap_ref, lag_ref, windows_ref, out_ref):
    step = pl.program_id(0)

    @pl.when(step == 0)
    def _():
        out_ref[...] = jnp.zeros_like(out_ref)

    def piece(b, k, place, plane):
        def lags(voxels):
            kept = lag_ref[plane, b, place : place + 1, voxels]
            if place == 1:
                return kept
            return jnp.where(swap_ref[step * group + b] == 1, lag_ref[plane, b, 1:2, voxels], kept)

        return (lambda: windows_ref[b, k]), lags

    add_pieces([piece(b, k, *unit) for b in range(group) for k, unit in enumerate(FIRST)], out_ref)


def first_beam(group, swap, lags, windows):
    planes, blocks, slots, voxels = lags.shape
    units = len(FIRST)

    def kernel(*refs):
        first_beam_kernel(group, *refs)

    return pl.pallas_call(
        kernel,
        grid_spec=pltpu.PrefetchScalarGridSpec(
            num_scalar_prefetch=1,
            grid=(blocks // group,),
            in_specs=[
                pl.BlockSpec((planes, group, slots, voxels), lambda i, *_: (0, i, 0, 0)),
                pl.BlockSpec((group, units, 128, 128), lambda i, *_: (i, 0, 0, 0)),
            ],
            out_specs=pl.BlockSpec((128, voxels), lambda i, *_: (0, 0)),
        ),
        out_shape=jax.ShapeDtypeStruct((128, voxels), F32),
        compiler_params=pltpu.CompilerParams(vmem_limit_bytes=62_000_000),
        cost_estimate=pl.CostEstimate(
            flops=2 * 128 * voxels * 128 * blocks * units,
            bytes_accessed=blocks * units * (128 * 256 + 8 * voxels),
            transcendentals=0,
        ),
        name="beam",
    )(swap, lags, windows)


def second_beam_kernel(
    list_ref, gain_ref, lag_ref, before_hbm, windows_hbm, out_ref, gram_ref, before_ref, held_ref, before_sem, sems
):
    ((place, plane),) = SECOND
    count = list_ref[lag_ref.shape[1]]
    groups = (count + LIST_GROUP - 1) // LIST_GROUP

    def fetches(group, half):
        return [
            pltpu.make_async_copy(
                windows_hbm.at[list_ref[group * LIST_GROUP + j], 0], held_ref.at[half, j], sems.at[half, j]
            )
            for j in range(LIST_GROUP)
        ]

    @pl.when(groups > 0)
    def _():
        for copy in fetches(0, 0):
            copy.start()

    before = pltpu.make_async_copy(before_hbm, before_ref, before_sem)
    before.start()
    out_ref[...] = jnp.zeros_like(out_ref)

    def one_group(group, carry):
        half = lax.rem(group, 2)

        @pl.when(group + 1 < groups)
        def _():
            for copy in fetches(group + 1, 1 - half):
                copy.start()

        for copy in fetches(group, half):
            copy.wait()

        def piece(j):
            block = list_ref[group * LIST_GROUP + j]
            return (lambda: held_ref[half, j]), (lambda voxels: lag_ref[plane, block, place : place + 1, voxels])

        add_pieces([piece(j) for j in range(LIST_GROUP)], out_ref)
        return carry

    lax.fori_loop(0, groups, one_group, 0)

    before.wait()
    beam = (before_ref[...] + out_ref[...]) * gain_ref[0]
    out_ref[...] = beam
    high = beam.astype(BF)
    rest = beam - high.astype(F32)
    middle = rest.astype(BF)
    low = (rest - middle.astype(F32)).astype(BF)
    dims = (((1,), (1,)), ((), ()))
    stacked = jnp.concatenate([high, middle], axis=0)
    main = lax.dot_general(stacked, stacked, dims, preferred_element_type=F32)
    cross = main[:128, 128:] + lax.dot_general(high, low, dims, preferred_element_type=F32)
    gram_ref[...] = main[:128, :128] + (cross + cross.T + main[128:, 128:])


def second_beam(order, gain, lags, windows, before):
    planes, blocks, slots, voxels = lags.shape
    smem, vmem = pl.BlockSpec(memory_space=pltpu.SMEM), pl.BlockSpec(memory_space=pltpu.VMEM)
    return pl.pallas_call(
        second_beam_kernel,
        in_specs=[smem, smem, vmem] + [pl.BlockSpec(memory_space=pltpu.HBM)] * 2,
        out_specs=[vmem, vmem],
        out_shape=[jax.ShapeDtypeStruct((128, voxels), F32), jax.ShapeDtypeStruct((128, 128), F32)],
        scratch_shapes=[
            pltpu.VMEM((128, voxels), F32),
            pltpu.VMEM((2, LIST_GROUP, 128, 128), BF),
            pltpu.SemaphoreType.DMA,
            pltpu.SemaphoreType.DMA((2, LIST_GROUP)),
        ],
        compiler_params=pltpu.CompilerParams(vmem_limit_bytes=40 * 2**20),
        cost_estimate=pl.CostEstimate(
            flops=2 * 128 * voxels * 128 * blocks,
            bytes_accessed=blocks * (128 * 256 + 8 * voxels),
            transcendentals=0,
        ),
        name="beam",
    )(order, gain, lags, before, windows)


def live_order(seen):
    blocks = seen.shape[0]
    swap = ((seen[:, 0] < 0) & (seen[:, 1] >= 0)).astype(jnp.int32)
    key = 1 - ((seen[:, 0] >= 0) & (seen[:, 1] >= 0)).astype(jnp.int32)
    ids = jnp.arange(blocks, dtype=jnp.int32)
    key = key * blocks + ids
    rank = jnp.sum((key[None, :] < key[:, None]).astype(jnp.int32), axis=1)
    order = jnp.sum(jnp.where(rank[None, :] == ids[:, None], ids[None, :], 0), axis=1)
    count = jnp.sum((key < blocks).astype(jnp.int32), keepdims=True)
    return swap, jnp.concatenate([order, count])


def product2(x, y):
    return [[x[i][0] * y[0][j] + x[i][1] * y[1][j] for j in range(2)] for i in range(2)]


def inverse2(x):
    over = 1.0 / (x[0][0] * x[1][1] - x[0][1] * x[1][0])
    return [[x[1][1] * over, -x[0][1] * over], [-x[1][0] * over, x[0][0] * over]]


def inverse4(p):
    e, f, g, h = ([[p[r + i][c + j] for j in range(2)] for i in range(2)] for r in (0, 2) for c in (0, 2))
    e = inverse2(e)
    ge, ef = product2(g, e), product2(e, f)
    t = product2(g, ef)
    s = inverse2([[h[i][j] - t[i][j] for j in range(2)] for i in range(2)])
    right, left = product2(ef, s), product2(s, ge)
    t = product2(right, ge)
    top = [[e[i][0] + t[i][0], e[i][1] + t[i][1], -right[i][0], -right[i][1]] for i in range(2)]
    return top + [[-left[i][0], -left[i][1], s[i][0], s[i][1]] for i in range(2)]


def invert(a):
    n = a.shape[0]
    lane = lax.broadcasted_iota(jnp.int32, (n, n), 1)
    lane_row = lane[:1]
    sub = lax.broadcasted_iota(jnp.int32, (8, n), 0)
    for k in range(0, n, 4):
        rows = [a[k + i : k + i + 1, :] for i in range(4)]
        cols = [jnp.broadcast_to(a[:, k + i : k + i + 1], (n, n)) for i in range(4)]
        pivot = inverse4([[cols[j][k + i : k + i + 1] for j in range(4)] for i in range(4)])
        new = []
        for i in range(4):
            q = pivot[i]
            row = (q[0] * rows[0] + q[1] * rows[1]) + (q[2] * rows[2] + q[3] * rows[3])
            for j in range(4):
                row = jnp.where(lane_row == k + j, q[j], row)
            new.append(row)
        update = (cols[0] * new[0] + cols[1] * new[1]) + (cols[2] * new[2] + cols[3] * new[3])
        a = jnp.where((lane >= k) & (lane < k + 4), 0.0, a) - update
        g = k // 8 * 8
        fixed = a[g : g + 8]
        for i in range(4):
            fixed = jnp.where(sub == k + i - g, new[i], fixed)
        a = jnp.concatenate([part for part in (a[:g], fixed, a[g + 8 :]) if part.shape[0]], axis=0)
    return a


def power_kernel(samples, gram_ref, beam_ref, out_ref):
    n = gram_ref.shape[0]
    gram = gram_ref[...]
    eye = lax.broadcasted_iota(jnp.int32, (n, n), 0) == lax.broadcasted_iota(jnp.int32, (n, n), 1)
    energy = jnp.sum(jnp.where(eye, gram, 0.0), keepdims=True)
    correlation = gram * (n / energy)
    filter_matrix = damping * invert(correlation + jnp.where(eye, damping, 0.0))
    filtered = lax.dot_general(
        filter_matrix,
        beam_ref[...],
        (((0,), (0,)), ((), ())),
        precision=lax.Precision.HIGHEST,
        preferred_element_type=F32,
    ) / jnp.sqrt(energy / samples)
    out_ref[...] = jnp.log(jnp.sum(filtered * filtered, axis=0, keepdims=True) / n + 1e-06)


def doppler_power(samples, gram, beam):
    def kernel(*refs):
        power_kernel(samples, *refs)

    return pl.pallas_call(
        kernel,
        out_shape=jax.ShapeDtypeStruct((1, beam.shape[1]), F32),
        compiler_params=pltpu.CompilerParams(vmem_limit_bytes=48 * 2**20),
        name="power",
    )(gram, beam)


def exchange_sum(x):
    for axis, digits in (("elem", (1,)), ("elem", (2, 4, 6)), ("vox", (1, 2, 3)), ("vox", (4, 8, 12))):
        size = lax.axis_size(axis)
        parts = [lax.ppermute(x, axis, [(i, i ^ k) for i in range(size)]) for k in digits]
        for part in parts:
            x = x + part
    return x


def shards(echoes, filter_taps, visible, window_start, delays, tile_gain):
    members, planes, frames, samples = echoes.shape
    channels = 2 * frames
    device_count = lax.axis_size("elem") * lax.axis_size("vox")
    voxels = delays.shape[-1]

    seen = jnp.transpose(visible, (0, 2, 1)).reshape(-1, visible.shape[1])
    starts = jnp.transpose(window_start[:, :, 0, :], (0, 2, 1)).reshape(-1, window_start.shape[1])
    first, second = make_windows(echoes, filter_taps, seen, starts)

    first = lax.all_to_all(first, AXES, split_axis=0, concat_axis=0, tiled=True)
    second = lax.all_to_all(second, AXES, split_axis=0, concat_axis=0, tiled=True)
    visible, first = lax.optimization_barrier((visible, first))
    my_seen = lax.dynamic_index_in_dim(visible, lax.axis_index(AXES), 0, keepdims=False)
    swap, order = live_order(my_seen)
    lags = delays[:, 0]
    partial = first_beam(4, swap, lags, first)
    beam, local_gram = second_beam(order, tile_gain, lags, second, partial)

    frame_gram = exchange_sum(local_gram)
    return doppler_power(channels * device_count * voxels, frame_gram, beam)


def solution(mesh):
    placed = (
        P(AXES, None, None, None),
        P(),
        P(),
        P(None, None, AXES, None),
        P(None, AXES, None, None, None),
        P(AXES),
    )
    return jax.shard_map(
        shards, mesh=mesh, in_specs=placed, out_specs=P(AXES, None), check_vma=False
    )
```

```python
import jax
import jax.numpy as jnp
from jax import lax
from jax.experimental import pallas as pl
from jax.experimental.pallas import tpu as pltpu
from jax.sharding import PartitionSpec as P

W = 128
damping = 0.5
AXES = ("elem", "vox")
BF, F32 = jnp.bfloat16, jnp.float32

FIRST = ((0, 0), (0, 1), (1, 0))
SECOND = ((1, 1),)
TILES_PER_STEP = 32
MEMBERS_PER_STEP = 4
LIST_GROUP = 8
SPREAD = 64


def window_kernel(seen_hbm, start_ref, taps_ref, echo_ref, first_ref, second_ref, base_ref, band_ref, seen_ref, sem):
    step = pl.program_id(0)
    planes = echo_ref.shape[1]
    zeros = base_ref.shape[0] - 2
    demod_steps = zeros // (4 * planes * MEMBERS_PER_STEP)
    fetch = pltpu.make_async_copy(seen_hbm, seen_ref, sem)

    @pl.when(step == 0)
    def _():
        fetch.start()
        base_ref[zeros:, :, :] = jnp.zeros((2, 128, 128), F32)
        taps = taps_ref[...].astype(F32)
        offset = lax.broadcasted_iota(jnp.int32, (640, 128), 0) - 4 * lax.broadcasted_iota(jnp.int32, (640, 128), 1)
        for c in range(2):
            band = jnp.zeros((640, 128), F32)
            for k in range(taps.shape[1]):
                band = jnp.where(offset == k, taps[c : c + 1, k : k + 1], band)
            band_ref[:, 128 * c : 128 * c + 128] = band.astype(BF)

    @pl.when(step < demod_steps)
    def _():
        for m in range(MEMBERS_PER_STEP):
            rows = []
            for plane in range(planes):
                x = echo_ref[m, plane]
                x = jnp.concatenate([x, jnp.zeros((x.shape[0], 128), x.dtype)], axis=1)
                for j in range(4):
                    rows.append(x[:, 512 * j : 512 * j + 640])
            out = jnp.dot(jnp.concatenate(rows, axis=0), band_ref[...], preferred_element_type=F32)
            out = out.astype(BF).astype(F32)
            for plane in range(planes):
                for j in range(4):
                    r = 64 * (4 * plane + j)
                    part = (MEMBERS_PER_STEP * step + m) * (4 * planes) + (4 * plane + j)
                    base_ref[part, 0:64, :] = out[r : r + 64, 0:128]
                    base_ref[part, 64:128, :] = out[r : r + 64, 128:256]

    @pl.when(step == demod_steps)
    def _():
        fetch.wait()

    @pl.when(step >= demod_steps)
    def _():
        lane = lax.broadcasted_iota(jnp.int32, (128, 128), 1)
        me = lax.axis_index(AXES)
        for i in range(TILES_PER_STEP):
            tile = (step - demod_steps) * TILES_PER_STEP + i
            seen0 = seen_ref[tile * 2, me]
            seen1 = seen_ref[tile * 2 + 1, me]
            keep = seen0 >= 0
            seen_at = (jnp.where(keep, seen0, seen1), jnp.where(keep, seen1, -1))
            for ref, units in ((first_ref, FIRST), (second_ref, SECOND)):
                for k, (place, plane) in enumerate(units):
                    seen = seen_at[place]
                    start = start_ref[plane * 2 + 1, tile]
                    if place == 0:
                        start = jnp.where(keep, start_ref[plane * 2, tile], start)
                    part = seen * (4 * planes) + (4 * plane + lax.shift_right_logical(start, 7))
                    part = jnp.where(seen >= 0, part, zeros)
                    both = jnp.where(lane >= (start & 127), base_ref[part], base_ref[part + 1])
                    out = pltpu.roll(both, (0 - start) & 127, 1)
                    ref[i, k] = out.astype(BF)


def make_windows(echoes, taps, seen, starts):
    members, planes, frames, samples = echoes.shape
    tiles = starts.shape[1]
    demod_steps = members // MEMBERS_PER_STEP

    def out_map(i):
        return (jnp.maximum(i - demod_steps, 0), 0, 0, 0)

    return pl.pallas_call(
        window_kernel,
        grid=(demod_steps + tiles // TILES_PER_STEP,),
        in_specs=[
            pl.BlockSpec(memory_space=pl.ANY),
            pl.BlockSpec(memory_space=pltpu.SMEM),
            pl.BlockSpec(taps.shape, lambda i: (0, 0)),
            pl.BlockSpec(
                (MEMBERS_PER_STEP, planes, frames, samples), lambda i: (jnp.minimum(i, demod_steps - 1), 0, 0, 0)
            ),
        ],
        out_specs=[pl.BlockSpec((TILES_PER_STEP, len(units), 128, 128), out_map) for units in (FIRST, SECOND)],
        scratch_shapes=[
            pltpu.VMEM((4 * members * planes + 2, 128, 128), F32),
            pltpu.VMEM((640, 256), BF),
            pltpu.SMEM(seen.shape, jnp.int32),
            pltpu.SemaphoreType.DMA,
        ],
        out_shape=[jax.ShapeDtypeStruct((tiles, len(units), 128, 128), BF) for units in (FIRST, SECOND)],
        compiler_params=pltpu.CompilerParams(vmem_limit_bytes=60 * 2**20),
        cost_estimate=pl.CostEstimate(flops=2 * 10**9, bytes_accessed=20 * 2**20, transcendentals=0),
        name="windows",
    )(seen, starts, taps, echoes)


def weights(lag):
    lag = jnp.broadcast_to(lag.astype(F32) * 0.25 - 64.0, (16, lag.shape[1])).astype(BF)
    iota = lax.broadcasted_iota(jnp.int32, (16, 128), 0).astype(F32)
    one, zero = jnp.ones((), BF), jnp.zeros((), BF)
    columns = []
    for c in range(lag.shape[1] // 128):
        d = lag[:, 128 * c : 128 * c + 128]
        columns.append(
            jnp.concatenate(
                [jnp.maximum(one - jnp.abs(d - (iota + (16.0 * w - 64.0)).astype(BF)), zero) for w in range(8)], axis=0
            )
        )
    return jnp.concatenate(columns, axis=1)


def add_pieces(pieces, acc_ref):
    for at in range(0, len(pieces), 2):
        pair = pieces[at : at + 2]
        lhs = jnp.concatenate([windows() for windows, lags in pair], axis=1)
        for v in range(0, acc_ref.shape[1], 256):
            rhs = jnp.concatenate([weights(lags(slice(v, v + 256))) for windows, lags in pair], axis=0)
            acc_ref[:, v : v + 256] += jnp.dot(lhs, rhs, preferred_element_type=F32)


def first_beam_kernel(group, swap_ref, lag_ref, windows_ref, out_ref):
    step = pl.program_id(0)

    @pl.when(step == 0)
    def _():
        out_ref[...] = jnp.zeros_like(out_ref)

    def piece(b, k, place, plane):
        def lags(voxels):
            kept = lag_ref[plane, b, place : place + 1, voxels]
            if place == 1:
                return kept
            return jnp.where(swap_ref[step * group + b] == 1, lag_ref[plane, b, 1:2, voxels], kept)

        return (lambda: windows_ref[b, k]), lags

    add_pieces([piece(b, k, *unit) for b in range(group) for k, unit in enumerate(FIRST)], out_ref)


def first_beam(group, swap, lags, windows):
    planes, blocks, slots, voxels = lags.shape
    units = len(FIRST)

    def kernel(*refs):
        first_beam_kernel(group, *refs)

    return pl.pallas_call(
        kernel,
        grid_spec=pltpu.PrefetchScalarGridSpec(
            num_scalar_prefetch=1,
            grid=(blocks // group,),
            in_specs=[
                pl.BlockSpec((planes, group, slots, voxels), lambda i, *_: (0, i, 0, 0)),
                pl.BlockSpec((group, units, 128, 128), lambda i, *_: (i, 0, 0, 0)),
            ],
            out_specs=pl.BlockSpec((None, 128, voxels), lambda i, *_: (0, 0, 0)),
        ),
        out_shape=jax.ShapeDtypeStruct((SPREAD, 128, voxels), F32),
        compiler_params=pltpu.CompilerParams(vmem_limit_bytes=62_000_000),
        cost_estimate=pl.CostEstimate(
            flops=2 * 128 * voxels * 128 * blocks * units,
            bytes_accessed=blocks * units * (128 * 256 + 8 * voxels),
            transcendentals=0,
        ),
        name="beam",
    )(swap, lags, windows)


def second_beam_kernel(
    list_ref, gain_ref, lag_ref, before_hbm, windows_hbm, out_ref, gram_ref, before_ref, held_ref, before_sem, sems
):
    ((place, plane),) = SECOND
    count = list_ref[lag_ref.shape[1]]
    groups = (count + LIST_GROUP - 1) // LIST_GROUP

    def fetches(group, half):
        return [
            pltpu.make_async_copy(
                windows_hbm.at[list_ref[group * LIST_GROUP + j], 0], held_ref.at[half, j], sems.at[half, j]
            )
            for j in range(LIST_GROUP)
        ]

    @pl.when(groups > 0)
    def _():
        for copy in fetches(0, 0):
            copy.start()

    before = pltpu.make_async_copy(before_hbm.at[0], before_ref, before_sem)
    before.start()
    out_ref[...] = jnp.zeros_like(out_ref)

    def one_group(group, carry):
        half = lax.rem(group, 2)

        @pl.when(group + 1 < groups)
        def _():
            for copy in fetches(group + 1, 1 - half):
                copy.start()

        for copy in fetches(group, half):
            copy.wait()

        def piece(j):
            block = list_ref[group * LIST_GROUP + j]
            return (lambda: held_ref[half, j]), (lambda voxels: lag_ref[plane, block, place : place + 1, voxels])

        add_pieces([piece(j) for j in range(LIST_GROUP)], out_ref)
        return carry

    lax.fori_loop(0, groups, one_group, 0)

    before.wait()
    beam = (before_ref[...] + out_ref[...]) * gain_ref[0]
    out_ref[...] = beam
    high, middle, low = split(beam)
    dims = (((1,), (1,)), ((), ()))
    stacked = jnp.concatenate([high, middle], axis=0)
    main = lax.dot_general(stacked, stacked, dims, preferred_element_type=F32)
    cross = main[:128, 128:] + lax.dot_general(high, low, dims, preferred_element_type=F32)
    gram_ref[...] = main[:128, :128] + (cross + cross.T + main[128:, 128:])


def second_beam(order, gain, lags, windows, before):
    planes, blocks, slots, voxels = lags.shape
    smem, vmem = pl.BlockSpec(memory_space=pltpu.SMEM), pl.BlockSpec(memory_space=pltpu.VMEM)
    return pl.pallas_call(
        second_beam_kernel,
        in_specs=[smem, smem, vmem] + [pl.BlockSpec(memory_space=pltpu.HBM)] * 2,
        out_specs=[vmem, vmem],
        out_shape=[jax.ShapeDtypeStruct((128, voxels), F32), jax.ShapeDtypeStruct((128, 128), F32)],
        scratch_shapes=[
            pltpu.VMEM((128, voxels), F32),
            pltpu.VMEM((2, LIST_GROUP, 128, 128), BF),
            pltpu.SemaphoreType.DMA,
            pltpu.SemaphoreType.DMA((2, LIST_GROUP)),
        ],
        compiler_params=pltpu.CompilerParams(vmem_limit_bytes=40 * 2**20),
        cost_estimate=pl.CostEstimate(
            flops=2 * 128 * voxels * 128 * blocks,
            bytes_accessed=blocks * (128 * 256 + 8 * voxels),
            transcendentals=0,
        ),
        name="beam",
    )(order, gain, lags, before, windows)


def live_order(seen):
    blocks = seen.shape[0]
    swap = ((seen[:, 0] < 0) & (seen[:, 1] >= 0)).astype(jnp.int32)
    key = 1 - ((seen[:, 0] >= 0) & (seen[:, 1] >= 0)).astype(jnp.int32)
    ids = jnp.arange(blocks, dtype=jnp.int32)
    key = key * blocks + ids
    rank = jnp.sum((key[None, :] < key[:, None]).astype(jnp.int32), axis=1)
    order = jnp.sum(jnp.where(rank[None, :] == ids[:, None], ids[None, :], 0), axis=1)
    count = jnp.sum((key < blocks).astype(jnp.int32), keepdims=True)
    return swap, jnp.concatenate([order, count])


def product2(x, y):
    return [[x[i][0] * y[0][j] + x[i][1] * y[1][j] for j in range(2)] for i in range(2)]


def inverse2(x):
    over = 1.0 / (x[0][0] * x[1][1] - x[0][1] * x[1][0])
    return [[x[1][1] * over, -x[0][1] * over], [-x[1][0] * over, x[0][0] * over]]


def inverse4(p):
    e, f, g, h = ([[p[r + i][c + j] for j in range(2)] for i in range(2)] for r in (0, 2) for c in (0, 2))
    e = inverse2(e)
    ge, ef = product2(g, e), product2(e, f)
    t = product2(g, ef)
    s = inverse2([[h[i][j] - t[i][j] for j in range(2)] for i in range(2)])
    right, left = product2(ef, s), product2(s, ge)
    t = product2(right, ge)
    top = [[e[i][0] + t[i][0], e[i][1] + t[i][1], -right[i][0], -right[i][1]] for i in range(2)]
    return top + [[-left[i][0], -left[i][1], s[i][0], s[i][1]] for i in range(2)]


def invert(a):
    n = a.shape[0]
    lane = lax.broadcasted_iota(jnp.int32, (n, n), 1)
    lane_row = lane[:1]
    sub = lax.broadcasted_iota(jnp.int32, (8, n), 0)
    for k in range(0, n, 4):
        rows = [a[k + i : k + i + 1, :] for i in range(4)]
        cols = [jnp.broadcast_to(a[:, k + i : k + i + 1], (n, n)) for i in range(4)]
        pivot = inverse4([[cols[j][k + i : k + i + 1] for j in range(4)] for i in range(4)])
        new = []
        for i in range(4):
            q = pivot[i]
            row = (q[0] * rows[0] + q[1] * rows[1]) + (q[2] * rows[2] + q[3] * rows[3])
            for j in range(4):
                row = jnp.where(lane_row == k + j, q[j], row)
            new.append(row)
        update = (cols[0] * new[0] + cols[1] * new[1]) + (cols[2] * new[2] + cols[3] * new[3])
        a = jnp.where((lane >= k) & (lane < k + 4), 0.0, a) - update
        g = k // 8 * 8
        fixed = a[g : g + 8]
        for i in range(4):
            fixed = jnp.where(sub == k + i - g, new[i], fixed)
        a = jnp.concatenate([part for part in (a[:g], fixed, a[g + 8 :]) if part.shape[0]], axis=0)
    return a


def split(x):
    high = x.astype(BF)
    rest = x - high.astype(F32)
    middle = rest.astype(BF)
    return high, middle, (rest - middle.astype(F32)).astype(BF)


def power_kernel(samples, gram_ref, beam_ref, out_ref):
    n = gram_ref.shape[0]
    gram = gram_ref[...]
    eye = lax.broadcasted_iota(jnp.int32, (n, n), 0) == lax.broadcasted_iota(jnp.int32, (n, n), 1)
    energy = jnp.sum(jnp.where(eye, gram, 0.0), keepdims=True)
    correlation = gram * (n / energy)
    beam = split(beam_ref[...])
    filter_matrix = split(damping * invert(correlation + jnp.where(eye, damping, 0.0)))
    filtered = jnp.zeros(beam_ref.shape, F32)
    for pair in (((1, 1), (0, 2)), ((2, 0), (1, 0)), ((0, 1), (0, 0))):
        lhs = jnp.concatenate([filter_matrix[i] for i, j in pair], axis=1)
        rhs = jnp.concatenate([beam[j] for i, j in pair], axis=0)
        filtered = filtered + jnp.dot(lhs, rhs, preferred_element_type=F32)
    filtered = filtered / jnp.sqrt(energy / samples)
    out_ref[...] = jnp.log(jnp.sum(filtered * filtered, axis=0, keepdims=True) / n + 1e-06)


def doppler_power(samples, gram, beam):
    def kernel(*refs):
        power_kernel(samples, *refs)

    return pl.pallas_call(
        kernel,
        out_shape=jax.ShapeDtypeStruct((1, beam.shape[1]), F32),
        compiler_params=pltpu.CompilerParams(vmem_limit_bytes=48 * 2**20),
        name="power",
    )(gram, beam)


def exchange_sum(x):
    for axis, digits in (("elem", (1,)), ("elem", (2, 4, 6)), ("vox", (1, 2, 3)), ("vox", (4, 8, 12))):
        size = lax.axis_size(axis)
        parts = [lax.ppermute(x, axis, [(i, i ^ k) for i in range(size)]) for k in digits]
        for part in parts:
            x = x + part
    return x


def shards(echoes, filter_taps, visible, window_start, delays, tile_gain):
    members, planes, frames, samples = echoes.shape
    channels = 2 * frames
    device_count = lax.axis_size("elem") * lax.axis_size("vox")
    voxels = delays.shape[-1]

    seen = jnp.transpose(visible, (0, 2, 1)).reshape(-1, visible.shape[1])
    starts = jnp.transpose(window_start[:, :, 0, :], (0, 2, 1)).reshape(-1, window_start.shape[1])
    first, second = make_windows(echoes, filter_taps, seen, starts)

    first = lax.all_to_all(first, AXES, split_axis=0, concat_axis=0, tiled=True)
    second = lax.all_to_all(second, AXES, split_axis=0, concat_axis=0, tiled=True)
    visible, first = lax.optimization_barrier((visible, first))
    my_seen = lax.dynamic_index_in_dim(visible, lax.axis_index(AXES), 0, keepdims=False)
    swap, order = live_order(my_seen)
    lags = delays[:, 0]
    partial = first_beam(4, swap, lags, first)
    beam, local_gram = second_beam(order, tile_gain, lags, second, partial)

    frame_gram = exchange_sum(local_gram)
    return doppler_power(channels * device_count * voxels, frame_gram, beam)


def solution(mesh):
    placed = (
        P(AXES, None, None, None),
        P(),
        P(),
        P(None, None, AXES, None),
        P(None, AXES, None, None, None),
        P(AXES),
    )
    return jax.shard_map(
        shards, mesh=mesh, in_specs=placed, out_specs=P(AXES, None), check_vma=False
    )
```

```python
import jax
import jax.numpy as jnp
from jax import lax
from jax.experimental import pallas as pl
from jax.experimental.pallas import tpu as pltpu
from jax.sharding import PartitionSpec as P

W = 128
damping = 0.5
AXES = ("elem", "vox")
BF, F32 = jnp.bfloat16, jnp.float32

FIRST = ((0, 0), (0, 1), (1, 0))
SECOND = ((1, 1),)
TILES_PER_STEP = 32
MEMBERS_PER_STEP = 4
LIST_GROUP = 16
SPREAD = 64


def window_kernel(seen_hbm, start_ref, taps_ref, echo_ref, first_ref, second_ref, base_ref, band_ref, seen_ref, sem):
    step = pl.program_id(0)
    planes = echo_ref.shape[1]
    zeros = base_ref.shape[0] - 2
    demod_steps = zeros // (4 * planes * MEMBERS_PER_STEP)
    fetch = pltpu.make_async_copy(seen_hbm, seen_ref, sem)

    @pl.when(step == 0)
    def _():
        fetch.start()
        base_ref[zeros:, :, :] = jnp.zeros((2, 128, 128), F32)
        taps = taps_ref[...].astype(F32)
        offset = lax.broadcasted_iota(jnp.int32, (640, 128), 0) - 4 * lax.broadcasted_iota(jnp.int32, (640, 128), 1)
        for c in range(2):
            band = jnp.zeros((640, 128), F32)
            for k in range(taps.shape[1]):
                band = jnp.where(offset == k, taps[c : c + 1, k : k + 1], band)
            band_ref[:, 128 * c : 128 * c + 128] = band.astype(BF)

    @pl.when(step < demod_steps)
    def _():
        for m in range(MEMBERS_PER_STEP):
            rows = []
            for plane in range(planes):
                x = echo_ref[m, plane]
                x = jnp.concatenate([x, jnp.zeros((x.shape[0], 128), x.dtype)], axis=1)
                for j in range(4):
                    rows.append(x[:, 512 * j : 512 * j + 640])
            out = jnp.dot(jnp.concatenate(rows, axis=0), band_ref[...], preferred_element_type=F32)
            out = out.astype(BF).astype(F32)
            for plane in range(planes):
                for j in range(4):
                    r = 64 * (4 * plane + j)
                    part = (MEMBERS_PER_STEP * step + m) * (4 * planes) + (4 * plane + j)
                    base_ref[part, 0:64, :] = out[r : r + 64, 0:128]
                    base_ref[part, 64:128, :] = out[r : r + 64, 128:256]

    @pl.when(step == demod_steps)
    def _():
        fetch.wait()

    @pl.when(step >= demod_steps)
    def _():
        lane = lax.broadcasted_iota(jnp.int32, (128, 128), 1)
        me = lax.axis_index(AXES)
        for i in range(TILES_PER_STEP):
            tile = (step - demod_steps) * TILES_PER_STEP + i
            seen0 = seen_ref[tile * 2, me]
            seen1 = seen_ref[tile * 2 + 1, me]
            keep = seen0 >= 0
            seen_at = (jnp.where(keep, seen0, seen1), jnp.where(keep, seen1, -1))
            for ref, units in ((first_ref, FIRST), (second_ref, SECOND)):
                for k, (place, plane) in enumerate(units):
                    seen = seen_at[place]
                    start = start_ref[plane * 2 + 1, tile]
                    if place == 0:
                        start = jnp.where(keep, start_ref[plane * 2, tile], start)
                    part = seen * (4 * planes) + (4 * plane + lax.shift_right_logical(start, 7))
                    part = jnp.where(seen >= 0, part, zeros)
                    both = jnp.where(lane >= (start & 127), base_ref[part], base_ref[part + 1])
                    out = pltpu.roll(both, (0 - start) & 127, 1)
                    ref[i, k] = out.astype(BF)


def make_windows(echoes, taps, seen, starts):
    members, planes, frames, samples = echoes.shape
    tiles = starts.shape[1]
    demod_steps = members // MEMBERS_PER_STEP

    def out_map(i):
        return (jnp.maximum(i - demod_steps, 0), 0, 0, 0)

    return pl.pallas_call(
        window_kernel,
        grid=(demod_steps + tiles // TILES_PER_STEP,),
        in_specs=[
            pl.BlockSpec(memory_space=pl.ANY),
            pl.BlockSpec(memory_space=pltpu.SMEM),
            pl.BlockSpec(taps.shape, lambda i: (0, 0)),
            pl.BlockSpec(
                (MEMBERS_PER_STEP, planes, frames, samples), lambda i: (jnp.minimum(i, demod_steps - 1), 0, 0, 0)
            ),
        ],
        out_specs=[pl.BlockSpec((TILES_PER_STEP, len(units), 128, 128), out_map) for units in (FIRST, SECOND)],
        scratch_shapes=[
            pltpu.VMEM((4 * members * planes + 2, 128, 128), F32),
            pltpu.VMEM((640, 256), BF),
            pltpu.SMEM(seen.shape, jnp.int32),
            pltpu.SemaphoreType.DMA,
        ],
        out_shape=[jax.ShapeDtypeStruct((tiles, len(units), 128, 128), BF) for units in (FIRST, SECOND)],
        compiler_params=pltpu.CompilerParams(vmem_limit_bytes=60 * 2**20),
        cost_estimate=pl.CostEstimate(flops=2 * 10**9, bytes_accessed=20 * 2**20, transcendentals=0),
        name="windows",
    )(seen, starts, taps, echoes)


def weights(lag):
    lag = jnp.broadcast_to(lag.astype(F32) * 0.25 - 64.0, (16, lag.shape[1])).astype(BF)
    iota = lax.broadcasted_iota(jnp.int32, (16, 128), 0).astype(F32)
    one, zero = jnp.ones((), BF), jnp.zeros((), BF)
    columns = []
    for c in range(lag.shape[1] // 128):
        d = lag[:, 128 * c : 128 * c + 128]
        columns.append(
            jnp.concatenate(
                [jnp.maximum(one - jnp.abs(d - (iota + (16.0 * w - 64.0)).astype(BF)), zero) for w in range(8)], axis=0
            )
        )
    return jnp.concatenate(columns, axis=1)


def add_pieces(pieces, acc_ref):
    for at in range(0, len(pieces), 2):
        pair = pieces[at : at + 2]
        lhs = jnp.concatenate([windows() for windows, lags in pair], axis=1)
        for v in range(0, acc_ref.shape[1], 256):
            rhs = jnp.concatenate([weights(lags(slice(v, v + 256))) for windows, lags in pair], axis=0)
            acc_ref[:, v : v + 256] += jnp.dot(lhs, rhs, preferred_element_type=F32)


def first_beam_kernel(group, swap_ref, lag_ref, windows_ref, out_ref):
    step = pl.program_id(0)

    @pl.when(step == 0)
    def _():
        out_ref[...] = jnp.zeros_like(out_ref)

    def piece(b, k, place, plane):
        def lags(voxels):
            kept = lag_ref[plane, b, place : place + 1, voxels]
            if place == 1:
                return kept
            return jnp.where(swap_ref[step * group + b] == 1, lag_ref[plane, b, 1:2, voxels], kept)

        return (lambda: windows_ref[b, k]), lags

    add_pieces([piece(b, k, *unit) for b in range(group) for k, unit in enumerate(FIRST)], out_ref)


def first_beam(group, swap, lags, windows):
    planes, blocks, slots, voxels = lags.shape
    units = len(FIRST)

    def kernel(*refs):
        first_beam_kernel(group, *refs)

    return pl.pallas_call(
        kernel,
        grid_spec=pltpu.PrefetchScalarGridSpec(
            num_scalar_prefetch=1,
            grid=(blocks // group,),
            in_specs=[
                pl.BlockSpec((planes, group, slots, voxels), lambda i, *_: (0, i, 0, 0)),
                pl.BlockSpec((group, units, 128, 128), lambda i, *_: (i, 0, 0, 0)),
            ],
            out_specs=pl.BlockSpec((None, 128, voxels), lambda i, *_: (0, 0, 0)),
        ),
        out_shape=jax.ShapeDtypeStruct((SPREAD, 128, voxels), F32),
        compiler_params=pltpu.CompilerParams(vmem_limit_bytes=62_000_000),
        cost_estimate=pl.CostEstimate(
            flops=2 * 128 * voxels * 128 * blocks * units,
            bytes_accessed=blocks * units * (128 * 256 + 8 * voxels),
            transcendentals=0,
        ),
        name="beam",
    )(swap, lags, windows)


def second_beam_kernel(
    list_ref, gain_ref, lag_ref, before_hbm, windows_hbm, out_ref, gram_ref, before_ref, held_ref, before_sem, sems
):
    ((place, plane),) = SECOND
    count = list_ref[lag_ref.shape[1]]
    groups = (count + LIST_GROUP - 1) // LIST_GROUP

    def fetches(group, half):
        return [
            pltpu.make_async_copy(
                windows_hbm.at[list_ref[group * LIST_GROUP + j], 0], held_ref.at[half, j], sems.at[half, j]
            )
            for j in range(LIST_GROUP)
        ]

    @pl.when(groups > 0)
    def _():
        for copy in fetches(0, 0):
            copy.start()

    before = pltpu.make_async_copy(before_hbm.at[0], before_ref, before_sem)
    before.start()
    out_ref[...] = jnp.zeros_like(out_ref)

    def one_group(group, carry):
        half = lax.rem(group, 2)

        @pl.when(group + 1 < groups)
        def _():
            for copy in fetches(group + 1, 1 - half):
                copy.start()

        for copy in fetches(group, half):
            copy.wait()

        def piece(j):
            block = list_ref[group * LIST_GROUP + j]
            return (lambda: held_ref[half, j]), (lambda voxels: lag_ref[plane, block, place : place + 1, voxels])

        add_pieces([piece(j) for j in range(LIST_GROUP)], out_ref)
        return carry

    lax.fori_loop(0, groups, one_group, 0)

    before.wait()
    beam = (before_ref[...] + out_ref[...]) * gain_ref[0]
    out_ref[...] = beam
    high, middle, low = split(beam)
    dims = (((1,), (1,)), ((), ()))
    stacked = jnp.concatenate([high, middle], axis=0)
    main = lax.dot_general(stacked, stacked, dims, preferred_element_type=F32)
    cross = main[:128, 128:] + lax.dot_general(high, low, dims, preferred_element_type=F32)
    gram_ref[...] = main[:128, :128] + (cross + cross.T + main[128:, 128:])


def second_beam(order, gain, lags, windows, before):
    planes, blocks, slots, voxels = lags.shape
    smem, vmem = pl.BlockSpec(memory_space=pltpu.SMEM), pl.BlockSpec(memory_space=pltpu.VMEM)
    return pl.pallas_call(
        second_beam_kernel,
        in_specs=[smem, smem, vmem] + [pl.BlockSpec(memory_space=pltpu.HBM)] * 2,
        out_specs=[vmem, vmem],
        out_shape=[jax.ShapeDtypeStruct((128, voxels), F32), jax.ShapeDtypeStruct((128, 128), F32)],
        scratch_shapes=[
            pltpu.VMEM((128, voxels), F32),
            pltpu.VMEM((2, LIST_GROUP, 128, 128), BF),
            pltpu.SemaphoreType.DMA,
            pltpu.SemaphoreType.DMA((2, LIST_GROUP)),
        ],
        compiler_params=pltpu.CompilerParams(vmem_limit_bytes=40 * 2**20),
        cost_estimate=pl.CostEstimate(
            flops=2 * 128 * voxels * 128 * blocks,
            bytes_accessed=blocks * (128 * 256 + 8 * voxels),
            transcendentals=0,
        ),
        name="beam",
    )(order, gain, lags, before, windows)


def live_order(seen):
    blocks = seen.shape[0]
    swap = ((seen[:, 0] < 0) & (seen[:, 1] >= 0)).astype(jnp.int32)
    key = 1 - ((seen[:, 0] >= 0) & (seen[:, 1] >= 0)).astype(jnp.int32)
    ids = jnp.arange(blocks, dtype=jnp.int32)
    key = key * blocks + ids
    rank = jnp.sum((key[None, :] < key[:, None]).astype(jnp.int32), axis=1)
    order = jnp.sum(jnp.where(rank[None, :] == ids[:, None], ids[None, :], 0), axis=1)
    count = jnp.sum((key < blocks).astype(jnp.int32), keepdims=True)
    return swap, jnp.concatenate([order, count])


def product2(x, y):
    return [[x[i][0] * y[0][j] + x[i][1] * y[1][j] for j in range(2)] for i in range(2)]


def inverse2(x):
    over = 1.0 / (x[0][0] * x[1][1] - x[0][1] * x[1][0])
    return [[x[1][1] * over, -x[0][1] * over], [-x[1][0] * over, x[0][0] * over]]


def inverse4(p):
    e, f, g, h = ([[p[r + i][c + j] for j in range(2)] for i in range(2)] for r in (0, 2) for c in (0, 2))
    e = inverse2(e)
    ge, ef = product2(g, e), product2(e, f)
    t = product2(g, ef)
    s = inverse2([[h[i][j] - t[i][j] for j in range(2)] for i in range(2)])
    right, left = product2(ef, s), product2(s, ge)
    t = product2(right, ge)
    top = [[e[i][0] + t[i][0], e[i][1] + t[i][1], -right[i][0], -right[i][1]] for i in range(2)]
    return top + [[-left[i][0], -left[i][1], s[i][0], s[i][1]] for i in range(2)]


def invert(a):
    n = a.shape[0]
    lane = lax.broadcasted_iota(jnp.int32, (n, n), 1)
    lane_row = lane[:1]
    sub = lax.broadcasted_iota(jnp.int32, (8, n), 0)
    for k in range(0, n, 4):
        rows = [a[k + i : k + i + 1, :] for i in range(4)]
        cols = [jnp.broadcast_to(a[:, k + i : k + i + 1], (n, n)) for i in range(4)]
        pivot = inverse4([[cols[j][k + i : k + i + 1] for j in range(4)] for i in range(4)])
        new = []
        for i in range(4):
            q = pivot[i]
            row = (q[0] * rows[0] + q[1] * rows[1]) + (q[2] * rows[2] + q[3] * rows[3])
            for j in range(4):
                row = jnp.where(lane_row == k + j, q[j], row)
            new.append(row)
        update = (cols[0] * new[0] + cols[1] * new[1]) + (cols[2] * new[2] + cols[3] * new[3])
        a = jnp.where((lane >= k) & (lane < k + 4), 0.0, a) - update
        g = k // 8 * 8
        fixed = a[g : g + 8]
        for i in range(4):
            fixed = jnp.where(sub == k + i - g, new[i], fixed)
        a = jnp.concatenate([part for part in (a[:g], fixed, a[g + 8 :]) if part.shape[0]], axis=0)
    return a


def split(x):
    high = x.astype(BF)
    rest = x - high.astype(F32)
    middle = rest.astype(BF)
    return high, middle, (rest - middle.astype(F32)).astype(BF)


def power_kernel(samples, gram_ref, beam_ref, out_ref):
    n = gram_ref.shape[0]
    gram = gram_ref[...]
    eye = lax.broadcasted_iota(jnp.int32, (n, n), 0) == lax.broadcasted_iota(jnp.int32, (n, n), 1)
    energy = jnp.sum(jnp.where(eye, gram, 0.0), keepdims=True)
    correlation = gram * (n / energy)
    beam = split(beam_ref[...])
    filter_matrix = split(damping * invert(correlation + jnp.where(eye, damping, 0.0)))
    filtered = jnp.zeros(beam_ref.shape, F32)
    for pair in (((1, 1), (0, 2)), ((2, 0), (1, 0)), ((0, 1), (0, 0))):
        lhs = jnp.concatenate([filter_matrix[i] for i, j in pair], axis=1)
        rhs = jnp.concatenate([beam[j] for i, j in pair], axis=0)
        filtered = filtered + jnp.dot(lhs, rhs, preferred_element_type=F32)
    filtered = filtered / jnp.sqrt(energy / samples)
    out_ref[...] = jnp.log(jnp.sum(filtered * filtered, axis=0, keepdims=True) / n + 1e-06)


def doppler_power(samples, gram, beam):
    def kernel(*refs):
        power_kernel(samples, *refs)

    return pl.pallas_call(
        kernel,
        out_shape=jax.ShapeDtypeStruct((1, beam.shape[1]), F32),
        compiler_params=pltpu.CompilerParams(vmem_limit_bytes=48 * 2**20),
        name="power",
    )(gram, beam)


def exchange_sum(x):
    for axis, digits in (("elem", (1,)), ("elem", (2, 4, 6)), ("vox", (1, 2, 3)), ("vox", (4, 8, 12))):
        size = lax.axis_size(axis)
        parts = [lax.ppermute(x, axis, [(i, i ^ k) for i in range(size)]) for k in digits]
        for part in parts:
            x = x + part
    return x


def shards(echoes, filter_taps, visible, window_start, delays, tile_gain):
    members, planes, frames, samples = echoes.shape
    channels = 2 * frames
    device_count = lax.axis_size("elem") * lax.axis_size("vox")
    voxels = delays.shape[-1]

    seen = jnp.transpose(visible, (0, 2, 1)).reshape(-1, visible.shape[1])
    starts = jnp.transpose(window_start[:, :, 0, :], (0, 2, 1)).reshape(-1, window_start.shape[1])
    first, second = make_windows(echoes, filter_taps, seen, starts)

    first = lax.all_to_all(first, AXES, split_axis=0, concat_axis=0, tiled=True)
    second = lax.all_to_all(second, AXES, split_axis=0, concat_axis=0, tiled=True)
    visible, first = lax.optimization_barrier((visible, first))
    my_seen = lax.dynamic_index_in_dim(visible, lax.axis_index(AXES), 0, keepdims=False)
    swap, order = live_order(my_seen)
    lags = delays[:, 0]
    partial = first_beam(4, swap, lags, first)
    beam, local_gram = second_beam(order, tile_gain, lags, second, partial)

    frame_gram = exchange_sum(local_gram)
    return doppler_power(channels * device_count * voxels, frame_gram, beam)


def solution(mesh):
    placed = (
        P(AXES, None, None, None),
        P(),
        P(),
        P(None, None, AXES, None),
        P(None, AXES, None, None, None),
        P(AXES),
    )
    return jax.shard_map(
        shards, mesh=mesh, in_specs=placed, out_specs=P(AXES, None), check_vma=False
    )
```
